32 devices in a mesh: rep: 2 (over y), grp: 8 (over z, x), tp: 2 (over core).
Axes of the slice: x: 2, y: 2, z: 4, core: 2. Of those that a mesh axis runs over, the one named last changes fastest.
Arguments:
- counts: int32 [16], P(('rep', 'grp')), parts along dimension 0, may hold values from 1 to 8, as said below
- hop_offsets: int32 [128], P(('rep', 'grp')), parts along dimension 0, may hold values from -2 to 2, as said below
- write_pos: int32 [128], P(('rep', 'grp')), parts along dimension 0, may hold values from 0 to 123
- kv_cache: bfloat16 [128, 2, 128, 1024], P(('rep', 'grp'), None, None, 'tp'), parts along dimension 0, may hold values from -27 to 27
- queries: bfloat16 [128, 2, 8192], P(('rep', 'grp'), None, 'tp'), parts along dimension 0, may hold values from -6 to 6
- fresh_kv: bfloat16 [128, 2, 2, 1024], P(('rep', 'grp'), None, None, 'tp'), parts along dimension 0, may hold values from -6 to 6
Outputs:
- new_cache: bfloat16 [128, 2, 128, 1024], P(('rep', 'grp'), None, None, 'tp'), parts along dimension 0
- attended: bfloat16 [128, 2, 8192], P(('rep', 'grp'), None, 'tp'), parts along dimension 0
- served: int32 [16], P('rep'), parts along dimension 0
The draws below stay inside these ranges and needn't reach their ends.
There are 2 independent parts, one for each index of `rep`. The reference program is written for one: setup_inputs(seed, part) draws one part's arguments, and reference() takes and returns one part's arrays. A program takes and returns all parts, laid end to end along the dimension named above; each array names one. Nothing has to cross between parts.
Inputs may be any that keep to these rules, and one draw needn't show every extreme that they name: `counts`: live streams fill a group's first slots; some group holds 8 streams; groups that send hold 8 streams, the others 1 or 2. `hop_offsets`: zero for empty slots and staying streams. A group sends at most one stream with each offset, and no group holds more than 8 streams after the move; offsets -2 and 2 occur.
All inputs are finite; a program needn't handle non-finite values.
Results may differ from the reference program's by a relative error of at most 0.0049.
Values may be sent and summed in bfloat16 or wider, within the bound.
A program may use at most 64 MiB of HBM per device.

```python
import jax
import jax.numpy as jnp
from jax import lax

HEADS = 64
KV_HEADS = 8
HEAD_DIM = 128
SINK = 4
REACH = 2
CACHE = 128
SLOTS = 8
WINDOW = 124
GROUPS = 8
STREAMS = 64


def migration_plan(key):
    base_key = jax.random.fold_in(key, 5)
    key_first = jax.random.fold_in(base_key, 0)
    key_light = jax.random.fold_in(base_key, 2)
    key_order = jax.random.fold_in(base_key, 3)
    group_index = jnp.arange(GROUPS)
    first_heavy = jax.random.randint(key_first, (), 0, 5)
    residue = (group_index - first_heavy) % 5
    is_heavy = ((residue == 0) | (residue == 2)) & (group_index < GROUPS - 2)
    light_count = jax.random.randint(key_light, (GROUPS,), 1, 3)
    count_table = jnp.where(is_heavy, SLOTS, light_count).astype(jnp.int32)
    slot_index = jnp.arange(SLOTS)
    order_scores = jax.random.randint(key_order, (GROUPS, SLOTS), 0, 1 << 20) * SLOTS + slot_index[None, :]
    slot_order = jnp.argsort(order_scores, axis=1)
    hop_table = jnp.zeros((GROUPS, SLOTS), jnp.int32)
    offsets = [offset for offset in range(-REACH, REACH + 1) if offset != 0]
    for position, offset in enumerate(offsets):
        chosen = (slot_order[:, position:position + 1] == slot_index[None, :]) & is_heavy[:, None]
        hop_table = hop_table + jnp.where(chosen, offset, 0).astype(jnp.int32)
    return (count_table, hop_table.reshape(-1))


def draw_counts(key, part):
    return migration_plan(key)[0]


def draw_hop_offsets(key, part):
    return migration_plan(key)[1]


def draw_kv_cache(key, part):
    key_values = jax.random.fold_in(jax.random.fold_in(key, 21), 0)
    shape = (STREAMS, 2, CACHE, KV_HEADS * HEAD_DIM)
    values_drawn = jnp.clip(jax.random.normal(key_values, shape, jnp.float32), -6.0, 6.0)
    return values_drawn.astype(jnp.bfloat16)


def draw_queries(key, part):
    key_values = jax.random.fold_in(jax.random.fold_in(key, 31), 0)
    shape = (STREAMS, 2, HEADS * HEAD_DIM)
    values_drawn = jnp.clip(jax.random.normal(key_values, shape, jnp.float32), -6.0, 6.0)
    return values_drawn.astype(jnp.bfloat16)


def with_ends(drawn, key, low, top_value):
    shape = drawn.shape
    place = [jax.random.randint(jax.random.fold_in(key, axis), (), 0, shape[axis]) for axis in range(len(shape))]
    drawn = drawn.at[tuple(place)].set(low)
    longest = shape.index(max(shape))
    place[longest] = (place[longest] + 1) % shape[longest]
    return drawn.at[tuple(place)].set(top_value)


def steps_of(rng, dims, pieces, least, largest):
    gain = 1.0
    for axis_at, parts in pieces:
        steps = jax.random.uniform(jax.random.fold_in(jax.random.fold_in(rng, 6), axis_at), (parts,), jnp.float32, least / len(pieces), largest / len(pieces))
        gain = gain * jnp.repeat(jnp.exp(steps), dims[axis_at] // parts).reshape((-1,) + (1,) * (len(dims) - 1 - axis_at))
    return gain


def scatter_about(own_key, shape, width, most, cuts=(), kind=jnp.bfloat16):
    gain = steps_of(own_key, shape, cuts, -0.22, 0.18) if cuts else 1.0
    entries = jax.random.normal(own_key, shape, jnp.float32) * width * gain
    return jnp.minimum(jnp.maximum(entries, -most), most).astype(kind)


def setup_inputs(seed: int = 0, part: int = 0) -> dict:
    key_of = jax.random.split(jax.random.key(seed), 7)
    part_splits = jax.random.split(jax.random.fold_in(key_of[6], part), 7)
    counts = draw_counts(jax.random.fold_in(jax.random.fold_in(key_of[6], part), 71), part)
    hop_offsets = draw_hop_offsets(jax.random.fold_in(jax.random.fold_in(key_of[6], part), 71), part)
    write_pos = with_ends(jax.random.randint(part_splits[2], (STREAMS,), 0, WINDOW), jax.random.fold_in(part_splits[2], 1), 0, WINDOW - 1).astype(jnp.int32)
    kv_cache = draw_kv_cache(jax.random.fold_in(jax.random.fold_in(key_of[6], part), 71), part)
    queries = draw_queries(jax.random.fold_in(jax.random.fold_in(key_of[6], part), 71), part)
    fresh_kv = scatter_about(part_splits[5], (STREAMS, 2, 2, KV_HEADS * HEAD_DIM), 1.0, 6.0, ((0, 8), (3, 2)))
    return dict(counts=counts, hop_offsets=hop_offsets, write_pos=write_pos, kv_cache=kv_cache, queries=queries, fresh_kv=fresh_kv)


def decode_rows(cache_rows, positions, query_rows, fresh_rows):
    row_count, _, cache_len, kv_width = cache_rows.shape
    group_count = kv_width // HEAD_DIM
    head_count = query_rows.shape[-1] // HEAD_DIM
    group_size = head_count // group_count
    window = cache_len - SINK
    columns = jnp.arange(cache_len, dtype=jnp.int32)
    outputs = []
    current = cache_rows
    for step_index in range(2):
        target = (SINK + (positions + step_index) % window).astype(jnp.int32)
        row_hit = (columns[None, :] == target[:, None])[:, None, :, None]
        current = jnp.where(row_hit, fresh_rows[:, :, step_index][:, :, None, :], current)
        key_rows = current[:, 0].reshape(row_count, cache_len, group_count, HEAD_DIM).astype(jnp.float32)
        values = current[:, 1].reshape(row_count, cache_len, group_count, HEAD_DIM).astype(jnp.float32)
        query_now = query_rows[:, step_index].reshape(row_count, group_count, group_size, HEAD_DIM).astype(jnp.float32)
        scores = jnp.einsum("rgkd,rlgd->rgkl", query_now, key_rows, precision=lax.Precision.HIGHEST) * (HEAD_DIM ** -0.5)
        weights = jax.nn.softmax(scores, axis=-1).astype(jnp.bfloat16)
        mixed_heads = jnp.einsum("rgkl,rlgd->rgkd", weights.astype(jnp.float32), values, precision=lax.Precision.HIGHEST)
        outputs.append(mixed_heads.astype(jnp.bfloat16).reshape(row_count, head_count * HEAD_DIM))
    return current, jnp.stack(outputs, axis=1)


def reference(counts, hop_offsets, write_pos, kv_cache, queries, fresh_kv):
    slot_index = jnp.arange(SLOTS, dtype=jnp.int32)
    group_index = jnp.arange(GROUPS, dtype=jnp.int32)
    is_live = slot_index[None, :] < counts[:, None]
    moving = jnp.where(is_live, hop_offsets.reshape(GROUPS, SLOTS), 0).astype(jnp.int32)
    staying = is_live & (moving == 0)
    stay_rank = jnp.cumsum(staying.astype(jnp.int32), axis=1).astype(jnp.int32) - 1
    running = jnp.sum(staying.astype(jnp.int32), axis=1).astype(jnp.int32)
    stream_ids = group_index[:, None] * SLOTS + slot_index[None, :]
    dest_parts = [jnp.where(staying, stay_rank, -1).astype(jnp.int32)]
    source_parts = [stream_ids]
    offsets = [offset for offset in range(-REACH, REACH + 1) if offset != 0]
    for offset in offsets:
        chosen = moving == offset
        present = jnp.any(chosen, axis=1)
        picked = jnp.sum(jnp.where(chosen, slot_index[None, :], 0), axis=1).astype(jnp.int32)
        incoming = jnp.roll(present, offset)
        anchor = jnp.roll(group_index * SLOTS + picked, offset).astype(jnp.int32)
        dest_parts.append(jnp.where(incoming, running, -1).astype(jnp.int32)[:, None])
        source_parts.append(anchor[:, None])
        running = running + incoming.astype(jnp.int32)
    pool_dest = jnp.concatenate(dest_parts, axis=1)
    pool_source = jnp.concatenate(source_parts, axis=1)
    matches = pool_dest[:, None, :] == slot_index[None, :, None]
    filled = jnp.any(matches, axis=2).reshape(-1)
    source = jnp.sum(jnp.where(matches, pool_source[:, None, :], 0), axis=2).astype(jnp.int32).reshape(-1)
    placed = jnp.take(kv_cache, source, axis=0)
    placed_pos = jnp.take(write_pos, source).astype(jnp.int32)

    def per_group(operands):
        return decode_rows(operands[0], operands[1], operands[2], operands[3])

    shaped = (placed.reshape((GROUPS, SLOTS) + placed.shape[1:]),
              placed_pos.reshape(GROUPS, SLOTS),
              queries.reshape((GROUPS, SLOTS) + queries.shape[1:]),
              fresh_kv.reshape((GROUPS, SLOTS) + fresh_kv.shape[1:]))
    cache_out, attention_out = lax.map(per_group, shaped)
    cache_out = cache_out.reshape(kv_cache.shape)
    attention_out = attention_out.reshape(queries.shape)
    new_cache = jnp.where(filled[:, None, None, None], cache_out, jnp.zeros((), jnp.bfloat16))
    attended = jnp.where(filled[:, None, None], attention_out, jnp.zeros((), jnp.bfloat16))
    return new_cache, attended, running
```

```python
import functools

import jax
import jax.numpy as jnp
from jax import lax
from jax.experimental import pallas as pl
from jax.experimental.pallas import tpu as pltpu
from jax.sharding import PartitionSpec as P

HEAD_DIM = 128
SINK = 4
OFFSETS = (-2, -1, 1, 2)
PACK = 16


def exchange_kernel(n, counts_ref, hops_ref, pos_ref, kv_ref, arrived_ref, table_ref,
                    staged, meta, send_sem, recv_sem, meta_send, meta_recv, own_sem):
    me = lax.axis_index("grp")
    slots = kv_ref.shape[0]
    barrier = pltpu.get_barrier_semaphore()

    @pl.loop(1, n)
    def _(k):
        pl.semaphore_signal(barrier, inc=1, device_id={"grp": lax.rem(me + k, n)})

    live = counts_ref[0]
    stay = jnp.int32(0)
    picked = [jnp.int32(0) for _ in OFFSETS]
    position = [jnp.int32(-1) for _ in OFFSETS]
    for s in range(slots):
        hop = jnp.where(s < live, hops_ref[s], 0)
        stay = stay + jnp.where((s < live) & (hop == 0), 1, 0)
        for i, offset in enumerate(OFFSETS):
            hit = hop == offset
            picked[i] = jnp.where(hit, s, picked[i])
            position[i] = jnp.where(hit, pos_ref[s], position[i])
    lane = lax.broadcasted_iota(jnp.int32, (1, 128), 1)
    row = jnp.where(lane == 0, stay, 0)
    for i in range(len(OFFSETS)):
        row = jnp.where(lane == 1 + i, position[i], row)
    meta[...] = row
    for i in range(len(OFFSETS)):
        staged[i] = kv_ref[picked[i]]

    pl.semaphore_wait(barrier, n - 1)

    def meta_copy(k):
        return pltpu.make_async_remote_copy(
            src_ref=meta, dst_ref=table_ref.at[me], send_sem=meta_send.at[k],
            recv_sem=meta_recv.at[k], device_id={"grp": lax.rem(me + k, n)})

    copies = []
    for i, offset in enumerate(OFFSETS):
        copies.append(pltpu.make_async_remote_copy(
            src_ref=staged.at[i], dst_ref=arrived_ref.at[i], send_sem=send_sem.at[i],
            recv_sem=recv_sem.at[i], device_id={"grp": lax.rem(me + offset + n, n)}))

    @pl.loop(1, n)
    def _(k):
        meta_copy(k).start()

    for i in (0, 3, 1, 2):
        copies[i].start()
    own = pltpu.make_async_copy(meta, table_ref.at[me], own_sem)
    own.start()
    own.wait()

    @pl.loop(1, n)
    def _(k):
        meta_copy(k).wait()

    for copy in copies:
        copy.wait()


def exchange(n, counts, hops, pos, kv):
    many = len(OFFSETS)
    smem = pl.BlockSpec(memory_space=pltpu.SMEM)
    vmem = pl.BlockSpec(memory_space=pltpu.VMEM)
    hbm = pl.BlockSpec(memory_space=pl.ANY)
    dma = pltpu.SemaphoreType.DMA
    return pl.pallas_call(
        functools.partial(exchange_kernel, n),
        out_shape=(jax.ShapeDtypeStruct((many,) + kv.shape[1:], kv.dtype),
                   jax.ShapeDtypeStruct((n, 1, 128), jnp.int32)),
        in_specs=[smem, smem, smem, vmem],
        out_specs=(hbm, hbm),
        scratch_shapes=[pltpu.VMEM((many,) + kv.shape[1:], kv.dtype),
                        pltpu.VMEM((1, 128), jnp.int32),
                        dma((many,)), dma((many,)), dma((n,)), dma((n,)), dma(())],
        compiler_params=pltpu.CompilerParams(collective_id=0, has_side_effects=True),
        name="exchange",
    )(counts, hops, pos, kv)


def decode_kernel(n, counts_ref, hops_ref, pos_ref, table_ref, kv_ref, arrived_ref, q_ref, fresh_ref,
                  out_ref, heads_ref, served_ref,
                  buf, zeros, q_rows, o_rows, place_pos, in_sem, out_sem):
    me = lax.axis_index("grp")
    slots, _, cache_len, width = kv_ref.shape
    kv_heads = width // HEAD_DIM
    heads = q_ref.shape[-1] // HEAD_DIM
    rows = 2 * heads // kv_heads
    window = cache_len - SINK

    live = counts_ref[0]
    filled = jnp.int32(0)
    for s in range(slots):
        stays = (s < live) & (hops_ref[s] == 0)

        @pl.when(stays)
        def _(s=s, at=filled):
            place_pos[at] = pos_ref[s]
            pltpu.make_async_copy(kv_ref.at[s], buf.at[at], in_sem.at[at]).start()

        filled = filled + jnp.where(stays, 1, 0)
    for i, offset in enumerate(OFFSETS):
        position = table_ref[lax.rem(me - offset + n, n), 0, 1 + i]
        present = position >= 0

        @pl.when(present)
        def _(i=i, at=filled, position=position):
            place_pos[at] = position
            pltpu.make_async_copy(arrived_ref.at[i], buf.at[at], in_sem.at[at]).start()

        filled = filled + jnp.where(present, 1, 0)

    zeros[...] = jnp.zeros_like(zeros)

    @pl.loop(0, n)
    def _(g):
        total = table_ref[g, 0, 0]
        for i, offset in enumerate(OFFSETS):
            total = total + jnp.where(table_ref[lax.rem(g - offset + n, n), 0, 1 + i] >= 0, 1, 0)
        served_ref[g] = total

    @pl.loop(filled, slots)
    def _(j):
        heads_ref[j] = jnp.zeros(heads_ref.shape[1:], heads_ref.dtype)
        pltpu.make_async_copy(zeros, out_ref.at[j], out_sem.at[j]).start()

    column = lax.broadcasted_iota(jnp.int32, (rows, cache_len), 1)
    first = lax.rem(lax.broadcasted_iota(jnp.int32, (rows, cache_len), 0), 2) == 0
    sub = lax.broadcasted_iota(jnp.int32, (PACK, width), 0)

    @pl.loop(0, filled)
    def _(j):
        q = q_ref[j].astype(jnp.float32)
        for h in range(heads):
            q_rows[2 * h:2 * h + 2] = q[:, h * HEAD_DIM:(h + 1) * HEAD_DIM]
        pltpu.make_async_copy(kv_ref.at[0], buf.at[j], in_sem.at[j]).wait()
        position = place_pos[j]
        target = [SINK + lax.rem(position + t, window) for t in range(2)]
        old = []
        for c in range(2):
            fresh = fresh_ref[j, c].astype(jnp.float32)
            for t in range(2):
                base = pl.multiple_of((target[t] // PACK) * PACK, PACK)
                block = buf[j, c, pl.ds(base, PACK), :].astype(jnp.float32)
                hit = sub + base == target[t]
                if t == 1:
                    old.append(jnp.sum(jnp.where(hit, block, 0.0), axis=0, keepdims=True))
                buf[j, c, pl.ds(base, PACK), :] = jnp.where(hit, fresh[t:t + 1], block).astype(buf.dtype)
        pltpu.make_async_copy(buf.at[j], out_ref.at[j], out_sem.at[j]).start()
        stale = first & (column == target[1])
        for g in range(kv_heads):
            lanes = slice(g * HEAD_DIM, (g + 1) * HEAD_DIM)
            query = q_rows[g * rows:(g + 1) * rows]
            keys = buf[j, 0, :, lanes]
            values = buf[j, 1, :, lanes]
            scores = lax.dot_general(query.astype(jnp.bfloat16), keys, (((1,), (1,)), ((), ())),
                                     preferred_element_type=jnp.float32)
            before = jnp.sum(query * old[0][:, lanes], axis=1, keepdims=True)
            scores = jnp.where(stale, before, scores) * HEAD_DIM ** -0.5
            raised = jnp.exp(scores - jnp.max(scores, axis=1, keepdims=True))
            weights = (raised / jnp.sum(raised, axis=1, keepdims=True)).astype(jnp.bfloat16)
            wide = weights.astype(jnp.float32)
            kept = jnp.where(stale, 0.0, wide).astype(jnp.bfloat16)
            stale_weight = jnp.sum(jnp.where(stale, wide, 0.0), axis=1, keepdims=True)
            mixed = lax.dot_general(kept, values, (((1,), (0,)), ((), ())),
                                    preferred_element_type=jnp.float32)
            o_rows[g * rows:(g + 1) * rows] = mixed + stale_weight * old[1][:, lanes]
        for h in range(heads):
            heads_ref[j, :, h * HEAD_DIM:(h + 1) * HEAD_DIM] = o_rows[2 * h:2 * h + 2].astype(heads_ref.dtype)

    @pl.loop(0, slots)
    def _(j):
        pltpu.make_async_copy(zeros, out_ref.at[j], out_sem.at[j]).wait()


def decode(n, counts, hops, pos, table, kv, arrived, queries, fresh):
    smem = pl.BlockSpec(memory_space=pltpu.SMEM)
    vmem = pl.BlockSpec(memory_space=pltpu.VMEM)
    hbm = pl.BlockSpec(memory_space=pl.ANY)
    dma = pltpu.SemaphoreType.DMA
    slots = kv.shape[0]
    heads = queries.shape[-1] // HEAD_DIM
    return pl.pallas_call(
        functools.partial(decode_kernel, n),
        out_shape=(jax.ShapeDtypeStruct(kv.shape, kv.dtype),
                   jax.ShapeDtypeStruct(queries.shape, queries.dtype),
                   jax.ShapeDtypeStruct((n,), jnp.int32)),
        in_specs=[smem, smem, smem, smem, hbm, hbm, vmem, vmem],
        out_specs=(hbm, vmem, smem),
        scratch_shapes=[pltpu.VMEM(kv.shape, kv.dtype),
                        pltpu.VMEM(kv.shape[1:], kv.dtype),
                        pltpu.VMEM((2 * heads, HEAD_DIM), jnp.float32),
                        pltpu.VMEM((2 * heads, HEAD_DIM), jnp.float32),
                        pltpu.SMEM((slots,), jnp.int32),
                        dma((slots,)), dma((slots,))],
        name="decode",
    )(counts, hops, pos, table, kv, arrived, queries, fresh)


def solution(mesh):
    n = mesh.shape["grp"]

    def per_device(counts, hop_offsets, write_pos, kv_cache, queries, fresh_kv):
        arrived, table = exchange(n, counts, hop_offsets, write_pos, kv_cache)
        return decode(n, counts, hop_offsets, write_pos, table, kv_cache, arrived, queries, fresh_kv)

    return jax.shard_map(
        per_device,
        mesh=mesh,
        in_specs=(
            P(("rep", "grp")),
            P(("rep", "grp")),
            P(("rep", "grp")),
            P(("rep", "grp"), None, None, "tp"),
            P(("rep", "grp"), None, "tp"),
            P(("rep", "grp"), None, None, "tp"),
        ),
        out_specs=(P(("rep", "grp"), None, None, "tp"), P(("rep", "grp"), None, "tp"), P("rep")),
        check_vma=False,
    )
```

```python
import functools

import jax
import jax.numpy as jnp
from jax import lax
from jax.experimental import pallas as pl
from jax.experimental.pallas import tpu as pltpu
from jax.sharding import PartitionSpec as P

HEAD_DIM = 128
SINK = 4
OFFSETS = (-2, -1, 1, 2)
PACK = 16


def attend(pair, fresh_of, keys_of, values_of, target, q_rows, o_rows):
    heads = pair.shape[-1] // HEAD_DIM
    q = pair.astype(jnp.float32)
    for h in range(heads):
        q_rows[2 * h:2 * h + 2] = q[:, h * HEAD_DIM:(h + 1) * HEAD_DIM]
    fresh = [fresh_of(c).astype(jnp.float32) for c in range(2)]
    kv_heads = fresh[0].shape[-1] // HEAD_DIM
    rows = 2 * heads // kv_heads
    for g in range(kv_heads):
        lanes = slice(g * HEAD_DIM, (g + 1) * HEAD_DIM)
        query = q_rows[g * rows:(g + 1) * rows]
        keys, values = keys_of(lanes), values_of(lanes)
        column = lax.broadcasted_iota(jnp.int32, (rows, keys.shape[0]), 1)
        second = lax.rem(lax.broadcasted_iota(jnp.int32, (rows, keys.shape[0]), 0), 2) == 1
        hits = [column == target[0], (column == target[1]) & second]
        scores = lax.dot_general(query.astype(jnp.bfloat16), keys, (((1,), (1,)), ((), ())),
                                 preferred_element_type=jnp.float32)
        for t in range(2):
            now = jnp.sum(query * fresh[0][t:t + 1, lanes], axis=1, keepdims=True)
            scores = jnp.where(hits[t], now, scores)
        scores = scores * HEAD_DIM ** -0.5
        raised = jnp.exp(scores - jnp.max(scores, axis=1, keepdims=True))
        weights = (raised / jnp.sum(raised, axis=1, keepdims=True)).astype(jnp.bfloat16)
        wide = weights.astype(jnp.float32)
        kept = jnp.where(hits[0] | hits[1], 0.0, wide).astype(jnp.bfloat16)
        mixed = lax.dot_general(kept, values, (((1,), (0,)), ((), ())),
                                preferred_element_type=jnp.float32)
        for t in range(2):
            share = jnp.sum(jnp.where(hits[t], wide, 0.0), axis=1, keepdims=True)
            mixed = mixed + share * fresh[1][t:t + 1, lanes]
        o_rows[g * rows:(g + 1) * rows] = mixed


def put_heads(ref, j, o_rows):
    for h in range(ref.shape[-1] // HEAD_DIM):
        ref[j, :, h * HEAD_DIM:(h + 1) * HEAD_DIM] = o_rows[2 * h:2 * h + 2].astype(ref.dtype)


def exchange_kernel(n, counts_ref, hops_ref, pos_ref, kv_hbm, q_ref, fresh_ref, arrived_ref, table_ref, local_ref,
                    kv_ref, staged, meta, q_rows, o_rows, dest, load_sem, send_sem, recv_sem, meta_send, meta_recv,
                    own_sem):
    me = lax.axis_index("grp")
    slots = kv_ref.shape[0]
    barrier = pltpu.get_barrier_semaphore()

    @pl.loop(1, n)
    def _(k):
        pl.semaphore_signal(barrier, inc=1, device_id={"grp": lax.rem(me + k, n)})

    load = pltpu.make_async_copy(kv_hbm, kv_ref, load_sem)
    load.start()
    live = counts_ref[0]
    stay = jnp.int32(0)
    picked = [jnp.int32(0) for _ in OFFSETS]
    position = [jnp.int32(-1) for _ in OFFSETS]
    for s in range(slots):
        hop = jnp.where(s < live, hops_ref[s], 0)
        dest[s] = stay
        stay = stay + jnp.where((s < live) & (hop == 0), 1, 0)
        for i, offset in enumerate(OFFSETS):
            hit = hop == offset
            picked[i] = jnp.where(hit, s, picked[i])
            position[i] = jnp.where(hit, pos_ref[s], position[i])
    lane = lax.broadcasted_iota(jnp.int32, (1, 128), 1)
    row = jnp.where(lane == 0, stay, 0)
    for i in range(len(OFFSETS)):
        row = jnp.where(lane == 1 + i, position[i], row)
    meta[...] = row
    load.wait()
    for i in range(len(OFFSETS)):
        staged[i] = kv_ref[picked[i]]

    pl.semaphore_wait(barrier, n - 1)

    def meta_copy(k):
        return pltpu.make_async_remote_copy(
            src_ref=meta, dst_ref=table_ref.at[me], send_sem=meta_send.at[k],
            recv_sem=meta_recv.at[k], device_id={"grp": lax.rem(me + k, n)})

    copies = []
    for i, offset in enumerate(OFFSETS):
        copies.append(pltpu.make_async_remote_copy(
            src_ref=staged.at[i], dst_ref=arrived_ref.at[i], send_sem=send_sem.at[i],
            recv_sem=recv_sem.at[i], device_id={"grp": lax.rem(me + offset + n, n)}))

    @pl.loop(1, n)
    def _(k):
        meta_copy(k).start()

    for i in (0, 3, 1, 2):
        copies[i].start()
    own = pltpu.make_async_copy(meta, table_ref.at[me], own_sem)
    own.start()
    window = kv_ref.shape[2] - SINK

    @pl.loop(0, slots)
    def _(s):
        at = jnp.minimum(dest[s], slots - 1)
        position = pos_ref[s]
        target = [SINK + lax.rem(position + t, window) for t in range(2)]
        attend(q_ref[at], lambda c: fresh_ref[at, c], lambda lanes: kv_ref[s, 0, :, lanes],
               lambda lanes: kv_ref[s, 1, :, lanes], target, q_rows, o_rows)
        put_heads(local_ref, s, o_rows)

    own.wait()

    @pl.loop(1, n)
    def _(k):
        meta_copy(k).wait()

    for copy in copies:
        copy.wait()


def exchange(n, counts, hops, pos, kv, queries, fresh):
    many = len(OFFSETS)
    heads = queries.shape[-1] // HEAD_DIM
    smem = pl.BlockSpec(memory_space=pltpu.SMEM)
    vmem = pl.BlockSpec(memory_space=pltpu.VMEM)
    hbm = pl.BlockSpec(memory_space=pl.ANY)
    dma = pltpu.SemaphoreType.DMA
    return pl.pallas_call(
        functools.partial(exchange_kernel, n),
        out_shape=(jax.ShapeDtypeStruct((many,) + kv.shape[1:], kv.dtype),
                   jax.ShapeDtypeStruct((n, 1, 128), jnp.int32),
                   jax.ShapeDtypeStruct(queries.shape, queries.dtype)),
        in_specs=[smem, smem, smem, hbm, vmem, vmem],
        out_specs=(hbm, hbm, vmem),
        scratch_shapes=[pltpu.VMEM(kv.shape, kv.dtype),
                        pltpu.VMEM((many,) + kv.shape[1:], kv.dtype),
                        pltpu.VMEM((1, 128), jnp.int32),
                        pltpu.VMEM((2 * heads, HEAD_DIM), jnp.float32),
                        pltpu.VMEM((2 * heads, HEAD_DIM), jnp.float32),
                        pltpu.SMEM((kv.shape[0],), jnp.int32),
                        dma(()), dma((many,)), dma((many,)), dma((n,)), dma((n,)), dma(())],
        compiler_params=pltpu.CompilerParams(collective_id=0, has_side_effects=True),
        name="exchange",
    )(counts, hops, pos, kv, queries, fresh)


def decode_kernel(n, counts_ref, hops_ref, pos_ref, table_ref, kv_ref, arrived_ref, q_ref, fresh_ref, local_ref,
                  out_ref, heads_ref, served_ref,
                  buf, raw, zeros, q_rows, o_rows, place_pos, in_sem, raw_sem, out_sem):
    me = lax.axis_index("grp")
    slots, _, cache_len, width = kv_ref.shape
    window = cache_len - SINK

    live = counts_ref[0]
    filled = jnp.int32(0)
    for s in range(slots):
        stays = (s < live) & (hops_ref[s] == 0)

        @pl.when(stays)
        def _(s=s, at=filled):
            place_pos[at] = pos_ref[s]
            pltpu.make_async_copy(kv_ref.at[s], buf.at[at], in_sem.at[at]).start()
            heads_ref[at] = local_ref[s]

        filled = filled + jnp.where(stays, 1, 0)
    stayed = filled
    for i, offset in enumerate(OFFSETS):
        position = table_ref[lax.rem(me - offset + n, n), 0, 1 + i]
        present = position >= 0

        @pl.when(present)
        def _(i=i, at=filled, position=position):
            place_pos[at] = position
            pltpu.make_async_copy(arrived_ref.at[i], buf.at[at], in_sem.at[at]).start()
            pltpu.make_async_copy(arrived_ref.at[i], raw.at[at - stayed], raw_sem.at[at - stayed]).start()

        filled = filled + jnp.where(present, 1, 0)

    zeros[...] = jnp.zeros_like(zeros)

    @pl.loop(0, n)
    def _(g):
        total = table_ref[g, 0, 0]
        for i, offset in enumerate(OFFSETS):
            total = total + jnp.where(table_ref[lax.rem(g - offset + n, n), 0, 1 + i] >= 0, 1, 0)
        served_ref[g] = total

    @pl.loop(filled, slots)
    def _(j):
        heads_ref[j] = jnp.zeros(heads_ref.shape[1:], heads_ref.dtype)
        pltpu.make_async_copy(zeros, out_ref.at[j], out_sem.at[j]).start()

    sub = lax.broadcasted_iota(jnp.int32, (PACK, width), 0)

    @pl.loop(0, filled)
    def _(j):
        pltpu.make_async_copy(kv_ref.at[0], buf.at[j], in_sem.at[j]).wait()
        position = place_pos[j]
        target = [SINK + lax.rem(position + t, window) for t in range(2)]
        for c in range(2):
            fresh = fresh_ref[j, c].astype(jnp.float32)
            for t in range(2):
                base = pl.multiple_of((target[t] // PACK) * PACK, PACK)
                block = buf[j, c, pl.ds(base, PACK), :].astype(jnp.float32)
                hit = sub + base == target[t]
                buf[j, c, pl.ds(base, PACK), :] = jnp.where(hit, fresh[t:t + 1], block).astype(buf.dtype)
        pltpu.make_async_copy(buf.at[j], out_ref.at[j], out_sem.at[j]).start()

    @pl.loop(stayed, filled)
    def _(j):
        k = j - stayed
        pltpu.make_async_copy(arrived_ref.at[0], raw.at[k], raw_sem.at[k]).wait()
        position = place_pos[j]
        target = [SINK + lax.rem(position + t, window) for t in range(2)]
        attend(q_ref[j], lambda c: fresh_ref[j, c], lambda lanes: raw[k, 0, :, lanes],
               lambda lanes: raw[k, 1, :, lanes], target, q_rows, o_rows)
        put_heads(heads_ref, j, o_rows)

    @pl.loop(0, slots)
    def _(j):
        pltpu.make_async_copy(zeros, out_ref.at[j], out_sem.at[j]).wait()


def decode(n, counts, hops, pos, table, kv, arrived, queries, fresh, local):
    smem = pl.BlockSpec(memory_space=pltpu.SMEM)
    vmem = pl.BlockSpec(memory_space=pltpu.VMEM)
    hbm = pl.BlockSpec(memory_space=pl.ANY)
    dma = pltpu.SemaphoreType.DMA
    slots = kv.shape[0]
    heads = queries.shape[-1] // HEAD_DIM
    return pl.pallas_call(
        functools.partial(decode_kernel, n),
        out_shape=(jax.ShapeDtypeStruct(kv.shape, kv.dtype),
                   jax.ShapeDtypeStruct(queries.shape, queries.dtype),
                   jax.ShapeDtypeStruct((n,), jnp.int32)),
        in_specs=[smem, smem, smem, smem, hbm, hbm, vmem, vmem, vmem],
        out_specs=(hbm, vmem, smem),
        scratch_shapes=[pltpu.VMEM(kv.shape, kv.dtype),
                        pltpu.VMEM(arrived.shape, kv.dtype),
                        pltpu.VMEM(kv.shape[1:], kv.dtype),
                        pltpu.VMEM((2 * heads, HEAD_DIM), jnp.float32),
                        pltpu.VMEM((2 * heads, HEAD_DIM), jnp.float32),
                        pltpu.SMEM((slots,), jnp.int32),
                        dma((slots,)), dma((len(OFFSETS),)), dma((slots,))],
        name="decode",
    )(counts, hops, pos, table, kv, arrived, queries, fresh, local)


def solution(mesh):
    n = mesh.shape["grp"]

    def per_device(counts, hop_offsets, write_pos, kv_cache, queries, fresh_kv):
        arrived, table, local = exchange(n, counts, hop_offsets, write_pos, kv_cache, queries, fresh_kv)
        return decode(n, counts, hop_offsets, write_pos, table, kv_cache, arrived, queries, fresh_kv, local)

    return jax.shard_map(
        per_device,
        mesh=mesh,
        in_specs=(
            P(("rep", "grp")),
            P(("rep", "grp")),
            P(("rep", "grp")),
            P(("rep", "grp"), None, None, "tp"),
            P(("rep", "grp"), None, "tp"),
            P(("rep", "grp"), None, None, "tp"),
        ),
        out_specs=(P(("rep", "grp"), None, None, "tp"), P(("rep", "grp"), None, "tp"), P("rep")),
        check_vma=False,
    )
```

```python
import functools

import jax
import jax.numpy as jnp
from jax import lax
from jax.experimental import pallas as pl
from jax.experimental.pallas import tpu as pltpu
from jax.sharding import PartitionSpec as P

HEAD_DIM = 128
SINK = 4
OFFSETS = (-2, -1, 1, 2)
PACK = 16


def attend(pair, fresh_of, keys_of, values_of, target, q_rows, o_rows):
    heads = pair.shape[-1] // HEAD_DIM
    q = pair.astype(jnp.float32)
    for h in range(heads):
        q_rows[2 * h:2 * h + 2] = q[:, h * HEAD_DIM:(h + 1) * HEAD_DIM]
    fresh = [fresh_of(c).astype(jnp.float32) for c in range(2)]
    kv_heads = fresh[0].shape[-1] // HEAD_DIM
    rows = 2 * heads // kv_heads
    for g in range(kv_heads):
        lanes = slice(g * HEAD_DIM, (g + 1) * HEAD_DIM)
        query = q_rows[g * rows:(g + 1) * rows]
        keys, values = keys_of(lanes), values_of(lanes)
        column = lax.broadcasted_iota(jnp.int32, (rows, keys.shape[0]), 1)
        second = lax.rem(lax.broadcasted_iota(jnp.int32, (rows, keys.shape[0]), 0), 2) == 1
        hits = [column == target[0], (column == target[1]) & second]
        scores = lax.dot_general(query.astype(jnp.bfloat16), keys, (((1,), (1,)), ((), ())),
                                 preferred_element_type=jnp.float32)
        for t in range(2):
            now = jnp.sum(query * fresh[0][t:t + 1, lanes], axis=1, keepdims=True)
            scores = jnp.where(hits[t], now, scores)
        scores = scores * HEAD_DIM ** -0.5
        raised = jnp.exp(scores - jnp.max(scores, axis=1, keepdims=True))
        weights = (raised / jnp.sum(raised, axis=1, keepdims=True)).astype(jnp.bfloat16)
        wide = weights.astype(jnp.float32)
        kept = jnp.where(hits[0] | hits[1], 0.0, wide).astype(jnp.bfloat16)
        mixed = lax.dot_general(kept, values, (((1,), (0,)), ((), ())),
                                preferred_element_type=jnp.float32)
        for t in range(2):
            share = jnp.sum(jnp.where(hits[t], wide, 0.0), axis=1, keepdims=True)
            mixed = mixed + share * fresh[1][t:t + 1, lanes]
        o_rows[g * rows:(g + 1) * rows] = mixed


def put_heads(ref, j, o_rows):
    for h in range(ref.shape[-1] // HEAD_DIM):
        ref[j, :, h * HEAD_DIM:(h + 1) * HEAD_DIM] = o_rows[2 * h:2 * h + 2].astype(ref.dtype)


def exchange_kernel(n, counts_ref, hops_ref, pos_ref, kv_hbm, q_hbm, fresh_hbm, arrived_ref, table_ref, local_ref,
                    kv_ref, q_ref, fresh_ref, staged, meta, q_rows, o_rows, dest, load_sem, send_sem, recv_sem, meta_send, meta_recv,
                    own_sem):
    me = lax.axis_index("grp")
    slots = kv_ref.shape[0]
    barrier = pltpu.get_barrier_semaphore()

    @pl.loop(1, n)
    def _(k):
        pl.semaphore_signal(barrier, inc=1, device_id={"grp": lax.rem(me + k, n)})

    load = pltpu.make_async_copy(kv_hbm, kv_ref, load_sem.at[0])
    load.start()
    others = [pltpu.make_async_copy(q_hbm, q_ref, load_sem.at[1]),
              pltpu.make_async_copy(fresh_hbm, fresh_ref, load_sem.at[2])]
    for other in others:
        other.start()
    live = counts_ref[0]
    stay = jnp.int32(0)
    picked = [jnp.int32(0) for _ in OFFSETS]
    position = [jnp.int32(-1) for _ in OFFSETS]
    for s in range(slots):
        hop = jnp.where(s < live, hops_ref[s], 0)
        dest[s] = stay
        stay = stay + jnp.where((s < live) & (hop == 0), 1, 0)
        for i, offset in enumerate(OFFSETS):
            hit = hop == offset
            picked[i] = jnp.where(hit, s, picked[i])
            position[i] = jnp.where(hit, pos_ref[s], position[i])
    lane = lax.broadcasted_iota(jnp.int32, (1, 128), 1)
    row = jnp.where(lane == 0, stay, 0)
    for i in range(len(OFFSETS)):
        row = jnp.where(lane == 1 + i, position[i], row)
    meta[...] = row
    load.wait()
    for i in range(len(OFFSETS)):
        staged[i] = kv_ref[picked[i]]

    pl.semaphore_wait(barrier, n - 1)

    def meta_copy(k):
        return pltpu.make_async_remote_copy(
            src_ref=meta, dst_ref=table_ref.at[me], send_sem=meta_send.at[k],
            recv_sem=meta_recv.at[k], device_id={"grp": lax.rem(me + k, n)})

    copies = []
    for i, offset in enumerate(OFFSETS):
        copies.append(pltpu.make_async_remote_copy(
            src_ref=staged.at[i], dst_ref=arrived_ref.at[i], send_sem=send_sem.at[i],
            recv_sem=recv_sem.at[i], device_id={"grp": lax.rem(me + offset + n, n)}))

    @pl.loop(1, n)
    def _(k):
        meta_copy(k).start()

    for i in (0, 3, 1, 2):
        copies[i].start()
    own = pltpu.make_async_copy(meta, table_ref.at[me], own_sem)
    own.start()
    for other in others:
        other.wait()
    window = kv_ref.shape[2] - SINK

    @pl.loop(0, slots)
    def _(s):
        at = jnp.minimum(dest[s], slots - 1)
        position = pos_ref[s]
        target = [SINK + lax.rem(position + t, window) for t in range(2)]
        attend(q_ref[at], lambda c: fresh_ref[at, c], lambda lanes: kv_ref[s, 0, :, lanes],
               lambda lanes: kv_ref[s, 1, :, lanes], target, q_rows, o_rows)
        put_heads(local_ref, s, o_rows)

    own.wait()

    @pl.loop(1, n)
    def _(k):
        meta_copy(k).wait()

    for copy in copies:
        copy.wait()


def exchange(n, counts, hops, pos, kv, queries, fresh):
    many = len(OFFSETS)
    heads = queries.shape[-1] // HEAD_DIM
    smem = pl.BlockSpec(memory_space=pltpu.SMEM)
    vmem = pl.BlockSpec(memory_space=pltpu.VMEM)
    hbm = pl.BlockSpec(memory_space=pl.ANY)
    dma = pltpu.SemaphoreType.DMA
    return pl.pallas_call(
        functools.partial(exchange_kernel, n),
        out_shape=(jax.ShapeDtypeStruct((many,) + kv.shape[1:], kv.dtype),
                   jax.ShapeDtypeStruct((n, 1, 128), jnp.int32),
                   jax.ShapeDtypeStruct(queries.shape, queries.dtype)),
        in_specs=[smem, smem, smem, hbm, hbm, hbm],
        out_specs=(hbm, hbm, vmem),
        scratch_shapes=[pltpu.VMEM(kv.shape, kv.dtype),
                        pltpu.VMEM(queries.shape, queries.dtype),
                        pltpu.VMEM(fresh.shape, fresh.dtype),
                        pltpu.VMEM((many,) + kv.shape[1:], kv.dtype),
                        pltpu.VMEM((1, 128), jnp.int32),
                        pltpu.VMEM((2 * heads, HEAD_DIM), jnp.float32),
                        pltpu.VMEM((2 * heads, HEAD_DIM), jnp.float32),
                        pltpu.SMEM((kv.shape[0],), jnp.int32),
                        dma((3,)), dma((many,)), dma((many,)), dma((n,)), dma((n,)), dma(())],
        compiler_params=pltpu.CompilerParams(collective_id=0, has_side_effects=True),
        name="exchange",
    )(counts, hops, pos, kv, queries, fresh)


def decode_kernel(n, counts_ref, hops_ref, pos_ref, table_ref, kv_ref, arrived_ref, q_ref, fresh_ref, local_ref,
                  out_ref, heads_ref, served_ref,
                  buf, raw, zeros, q_rows, o_rows, place_pos, in_sem, raw_sem, out_sem):
    me = lax.axis_index("grp")
    slots, _, cache_len, width = kv_ref.shape
    window = cache_len - SINK

    live = counts_ref[0]
    filled = jnp.int32(0)
    for s in range(slots):
        stays = (s < live) & (hops_ref[s] == 0)

        @pl.when(stays)
        def _(s=s, at=filled):
            place_pos[at] = pos_ref[s]
            pltpu.make_async_copy(kv_ref.at[s], buf.at[at], in_sem.at[at]).start()
            heads_ref[at] = local_ref[s]

        filled = filled + jnp.where(stays, 1, 0)
    stayed = filled
    for i, offset in enumerate(OFFSETS):
        position = table_ref[lax.rem(me - offset + n, n), 0, 1 + i]
        present = position >= 0

        @pl.when(present)
        def _(i=i, at=filled, position=position):
            place_pos[at] = position
            pltpu.make_async_copy(arrived_ref.at[i], buf.at[at], in_sem.at[at]).start()
            pltpu.make_async_copy(arrived_ref.at[i], raw.at[at - stayed], raw_sem.at[at - stayed]).start()

        filled = filled + jnp.where(present, 1, 0)

    zeros[...] = jnp.zeros_like(zeros)

    @pl.loop(0, n)
    def _(g):
        total = table_ref[g, 0, 0]
        for i, offset in enumerate(OFFSETS):
            total = total + jnp.where(table_ref[lax.rem(g - offset + n, n), 0, 1 + i] >= 0, 1, 0)
        served_ref[g] = total

    @pl.loop(filled, slots)
    def _(j):
        heads_ref[j] = jnp.zeros(heads_ref.shape[1:], heads_ref.dtype)
        pltpu.make_async_copy(zeros, out_ref.at[j], out_sem.at[j]).start()

    sub = lax.broadcasted_iota(jnp.int32, (PACK, width), 0)

    @pl.loop(0, filled)
    def _(j):
        pltpu.make_async_copy(kv_ref.at[0], buf.at[j], in_sem.at[j]).wait()
        position = place_pos[j]
        target = [SINK + lax.rem(position + t, window) for t in range(2)]
        for c in range(2):
            fresh = fresh_ref[j, c].astype(jnp.float32)
            for t in range(2):
                base = pl.multiple_of((target[t] // PACK) * PACK, PACK)
                block = buf[j, c, pl.ds(base, PACK), :].astype(jnp.float32)
                hit = sub + base == target[t]
                buf[j, c, pl.ds(base, PACK), :] = jnp.where(hit, fresh[t:t + 1], block).astype(buf.dtype)
        pltpu.make_async_copy(buf.at[j], out_ref.at[j], out_sem.at[j]).start()

    @pl.loop(stayed, filled)
    def _(j):
        k = j - stayed
        pltpu.make_async_copy(arrived_ref.at[0], raw.at[k], raw_sem.at[k]).wait()
        position = place_pos[j]
        target = [SINK + lax.rem(position + t, window) for t in range(2)]
        attend(q_ref[j], lambda c: fresh_ref[j, c], lambda lanes: raw[k, 0, :, lanes],
               lambda lanes: raw[k, 1, :, lanes], target, q_rows, o_rows)
        put_heads(heads_ref, j, o_rows)

    @pl.loop(0, slots)
    def _(j):
        pltpu.make_async_copy(zeros, out_ref.at[j], out_sem.at[j]).wait()


def decode(n, counts, hops, pos, table, kv, arrived, queries, fresh, local):
    smem = pl.BlockSpec(memory_space=pltpu.SMEM)
    vmem = pl.BlockSpec(memory_space=pltpu.VMEM)
    hbm = pl.BlockSpec(memory_space=pl.ANY)
    dma = pltpu.SemaphoreType.DMA
    slots = kv.shape[0]
    heads = queries.shape[-1] // HEAD_DIM
    return pl.pallas_call(
        functools.partial(decode_kernel, n),
        out_shape=(jax.ShapeDtypeStruct(kv.shape, kv.dtype),
                   jax.ShapeDtypeStruct(queries.shape, queries.dtype),
                   jax.ShapeDtypeStruct((n,), jnp.int32)),
        in_specs=[smem, smem, smem, smem, hbm, hbm, vmem, vmem, vmem],
        out_specs=(hbm, vmem, smem),
        scratch_shapes=[pltpu.VMEM(kv.shape, kv.dtype),
                        pltpu.VMEM(arrived.shape, kv.dtype),
                        pltpu.VMEM(kv.shape[1:], kv.dtype),
                        pltpu.VMEM((2 * heads, HEAD_DIM), jnp.float32),
                        pltpu.VMEM((2 * heads, HEAD_DIM), jnp.float32),
                        pltpu.SMEM((slots,), jnp.int32),
                        dma((slots,)), dma((len(OFFSETS),)), dma((slots,))],
        name="decode",
    )(counts, hops, pos, table, kv, arrived, queries, fresh, local)


def solution(mesh):
    n = mesh.shape["grp"]

    def per_device(counts, hop_offsets, write_pos, kv_cache, queries, fresh_kv):
        arrived, table, local = exchange(n, counts, hop_offsets, write_pos, kv_cache, queries, fresh_kv)
        return decode(n, counts, hop_offsets, write_pos, table, kv_cache, arrived, queries, fresh_kv, local)

    return jax.shard_map(
        per_device,
        mesh=mesh,
        in_specs=(
            P(("rep", "grp")),
            P(("rep", "grp")),
            P(("rep", "grp")),
            P(("rep", "grp"), None, None, "tp"),
            P(("rep", "grp"), None, "tp"),
            P(("rep", "grp"), None, None, "tp"),
        ),
        out_specs=(P(("rep", "grp"), None, None, "tp"), P(("rep", "grp"), None, "tp"), P("rep")),
        check_vma=False,
    )
```

```python
import functools

import jax
import jax.numpy as jnp
from jax import lax
from jax.experimental import pallas as pl
from jax.experimental.pallas import tpu as pltpu
from jax.sharding import PartitionSpec as P

HEAD_DIM = 128
SINK = 4
OFFSETS = (-2, -1, 1, 2)
PACK = 16


def attend(pair, fresh_of, keys_of, values_of, target, q_rows, o_rows):
    heads = pair.shape[-1] // HEAD_DIM
    q = pair.astype(jnp.float32)
    for h in range(heads):
        q_rows[2 * h:2 * h + 2] = q[:, h * HEAD_DIM:(h + 1) * HEAD_DIM]
    fresh = [fresh_of(c).astype(jnp.float32) for c in range(2)]
    kv_heads = fresh[0].shape[-1] // HEAD_DIM
    rows = 2 * heads // kv_heads
    for g in range(kv_heads):
        lanes = slice(g * HEAD_DIM, (g + 1) * HEAD_DIM)
        query = q_rows[g * rows:(g + 1) * rows]
        keys, values = keys_of(lanes), values_of(lanes)
        column = lax.broadcasted_iota(jnp.int32, (rows, keys.shape[0]), 1)
        second = lax.rem(lax.broadcasted_iota(jnp.int32, (rows, keys.shape[0]), 0), 2) == 1
        hits = [column == target[0], (column == target[1]) & second]
        scores = lax.dot_general(query.astype(jnp.bfloat16), keys, (((1,), (1,)), ((), ())),
                                 preferred_element_type=jnp.float32)
        for t in range(2):
            now = jnp.sum(query * fresh[0][t:t + 1, lanes], axis=1, keepdims=True)
            scores = jnp.where(hits[t], now, scores)
        scores = scores * HEAD_DIM ** -0.5
        raised = jnp.exp(scores - jnp.max(scores, axis=1, keepdims=True))
        weights = (raised / jnp.sum(raised, axis=1, keepdims=True)).astype(jnp.bfloat16)
        wide = weights.astype(jnp.float32)
        kept = jnp.where(hits[0] | hits[1], 0.0, wide).astype(jnp.bfloat16)
        mixed = lax.dot_general(kept, values, (((1,), (0,)), ((), ())),
                                preferred_element_type=jnp.float32)
        for t in range(2):
            share = jnp.sum(jnp.where(hits[t], wide, 0.0), axis=1, keepdims=True)
            mixed = mixed + share * fresh[1][t:t + 1, lanes]
        o_rows[g * rows:(g + 1) * rows] = mixed


def put_heads(ref, j, o_rows):
    for h in range(ref.shape[-1] // HEAD_DIM):
        ref[j, :, h * HEAD_DIM:(h + 1) * HEAD_DIM] = o_rows[2 * h:2 * h + 2].astype(ref.dtype)


def exchange_kernel(n, counts_ref, hops_ref, pos_ref, kv_hbm, q_hbm, fresh_hbm, arrived_ref, table_ref, local_ref,
                    kv_ref, q_ref, fresh_ref, staged, meta, q_rows, o_rows, dest, load_sem, send_sem, recv_sem, meta_send, meta_recv,
                    own_sem):
    me = lax.axis_index("grp")
    slots = kv_ref.shape[0]
    barrier = pltpu.get_barrier_semaphore()

    @pl.loop(1, n)
    def _(k):
        pl.semaphore_signal(barrier, inc=1, device_id={"grp": lax.rem(me + k, n)})

    load = pltpu.make_async_copy(kv_hbm, kv_ref, load_sem.at[0])
    load.start()
    others = [pltpu.make_async_copy(q_hbm, q_ref, load_sem.at[1]),
              pltpu.make_async_copy(fresh_hbm, fresh_ref, load_sem.at[2])]
    for other in others:
        other.start()
    live = counts_ref[0]
    stay = jnp.int32(0)
    picked = [jnp.int32(0) for _ in OFFSETS]
    position = [jnp.int32(-1) for _ in OFFSETS]
    for s in range(slots):
        hop = jnp.where(s < live, hops_ref[s], 0)
        dest[s] = stay
        stay = stay + jnp.where((s < live) & (hop == 0), 1, 0)
        for i, offset in enumerate(OFFSETS):
            hit = hop == offset
            picked[i] = jnp.where(hit, s, picked[i])
            position[i] = jnp.where(hit, pos_ref[s], position[i])
    lane = lax.broadcasted_iota(jnp.int32, (1, 128), 1)
    row = jnp.where(lane == 0, stay, 0)
    for i in range(len(OFFSETS)):
        row = jnp.where(lane == 1 + i, position[i], row)
    meta[...] = row
    load.wait()
    for i in range(len(OFFSETS)):
        staged[i] = kv_ref[picked[i]]

    pl.semaphore_wait(barrier, n - 1)

    def meta_copy(k):
        return pltpu.make_async_remote_copy(
            src_ref=meta, dst_ref=table_ref.at[me], send_sem=meta_send.at[k],
            recv_sem=meta_recv.at[k], device_id={"grp": lax.rem(me + k, n)})

    copies = []
    for i, offset in enumerate(OFFSETS):
        copies.append(pltpu.make_async_remote_copy(
            src_ref=staged.at[i], dst_ref=arrived_ref.at[i], send_sem=send_sem.at[i],
            recv_sem=recv_sem.at[i], device_id={"grp": lax.rem(me + offset + n, n)}))

    @pl.loop(1, n)
    def _(k):
        meta_copy(k).start()

    for i in (0, 3, 1, 2):
        copies[i].start()
    own = pltpu.make_async_copy(meta, table_ref.at[me], own_sem)
    own.start()
    for other in others:
        other.wait()
    window = kv_ref.shape[2] - SINK

    @pl.loop(0, slots)
    def _(s):
        at = jnp.minimum(dest[s], slots - 1)
        position = pos_ref[s]
        target = [SINK + lax.rem(position + t, window) for t in range(2)]
        attend(q_ref[at], lambda c: fresh_ref[at, c], lambda lanes: kv_ref[s, 0, :, lanes],
               lambda lanes: kv_ref[s, 1, :, lanes], target, q_rows, o_rows)
        put_heads(local_ref, s, o_rows)

    own.wait()

    @pl.loop(1, n)
    def _(k):
        meta_copy(k).wait()

    for copy in copies:
        copy.wait()


def exchange(n, counts, hops, pos, kv, queries, fresh):
    many = len(OFFSETS)
    heads = queries.shape[-1] // HEAD_DIM
    smem = pl.BlockSpec(memory_space=pltpu.SMEM)
    vmem = pl.BlockSpec(memory_space=pltpu.VMEM)
    hbm = pl.BlockSpec(memory_space=pl.ANY)
    dma = pltpu.SemaphoreType.DMA
    return pl.pallas_call(
        functools.partial(exchange_kernel, n),
        out_shape=(jax.ShapeDtypeStruct((many,) + kv.shape[1:], kv.dtype),
                   jax.ShapeDtypeStruct((n, 1, 128), jnp.int32),
                   jax.ShapeDtypeStruct(queries.shape, queries.dtype)),
        in_specs=[smem, smem, smem, hbm, hbm, hbm],
        out_specs=(hbm, hbm, vmem),
        scratch_shapes=[pltpu.VMEM(kv.shape, kv.dtype),
                        pltpu.VMEM(queries.shape, queries.dtype),
                        pltpu.VMEM(fresh.shape, fresh.dtype),
                        pltpu.VMEM((many,) + kv.shape[1:], kv.dtype),
                        pltpu.VMEM((1, 128), jnp.int32),
                        pltpu.VMEM((2 * heads, HEAD_DIM), jnp.float32),
                        pltpu.VMEM((2 * heads, HEAD_DIM), jnp.float32),
                        pltpu.SMEM((kv.shape[0],), jnp.int32),
                        dma((3,)), dma((many,)), dma((many,)), dma((n,)), dma((n,)), dma(())],
        compiler_params=pltpu.CompilerParams(collective_id=0, has_side_effects=True),
        name="exchange",
    )(counts, hops, pos, kv, queries, fresh)


def decode_kernel(n, counts_ref, hops_ref, pos_ref, table_ref, kv_ref, arrived_ref, q_hbm, fresh_hbm, local_ref,
                  out_ref, heads_out, served_ref,
                  buf, raw, zeros, q_ref, fresh_ref, heads_ref, q_rows, o_rows, place_pos,
                  in_sem, raw_sem, out_sem, load_sem, heads_in, heads_sem):
    me = lax.axis_index("grp")
    slots, _, cache_len, width = kv_ref.shape
    window = cache_len - SINK

    load_fresh = pltpu.make_async_copy(fresh_hbm, fresh_ref, load_sem.at[0])
    load_q = pltpu.make_async_copy(q_hbm, q_ref, load_sem.at[1])
    load_fresh.start()
    live = counts_ref[0]
    filled = jnp.int32(0)
    for s in range(slots):
        stays = (s < live) & (hops_ref[s] == 0)

        @pl.when(stays)
        def _(s=s, at=filled):
            place_pos[at] = pos_ref[s]
            pltpu.make_async_copy(kv_ref.at[s], buf.at[at], in_sem.at[at]).start()
            pltpu.make_async_copy(local_ref.at[s], heads_ref.at[at], heads_in.at[at]).start()

        filled = filled + jnp.where(stays, 1, 0)
    stayed = filled
    for i, offset in enumerate(OFFSETS):
        position = table_ref[lax.rem(me - offset + n, n), 0, 1 + i]
        present = position >= 0

        @pl.when(present)
        def _(i=i, at=filled, position=position):
            place_pos[at] = position
            pltpu.make_async_copy(arrived_ref.at[i], buf.at[at], in_sem.at[at]).start()
            pltpu.make_async_copy(arrived_ref.at[i], raw.at[at - stayed], raw_sem.at[at - stayed]).start()

        filled = filled + jnp.where(present, 1, 0)

    load_q.start()
    zeros[...] = jnp.zeros_like(zeros)

    @pl.loop(0, n)
    def _(g):
        total = table_ref[g, 0, 0]
        for i, offset in enumerate(OFFSETS):
            total = total + jnp.where(table_ref[lax.rem(g - offset + n, n), 0, 1 + i] >= 0, 1, 0)
        served_ref[g] = total

    @pl.loop(filled, slots)
    def _(j):
        heads_ref[j] = jnp.zeros(heads_ref.shape[1:], heads_ref.dtype)
        pltpu.make_async_copy(heads_ref.at[j], heads_out.at[j], heads_sem.at[j]).start()
        pltpu.make_async_copy(zeros, out_ref.at[j], out_sem.at[j]).start()

    load_fresh.wait()
    sub = lax.broadcasted_iota(jnp.int32, (PACK, width), 0)

    @pl.loop(0, filled)
    def _(j):
        pltpu.make_async_copy(kv_ref.at[0], buf.at[j], in_sem.at[j]).wait()
        position = place_pos[j]
        target = [SINK + lax.rem(position + t, window) for t in range(2)]
        for c in range(2):
            fresh = fresh_ref[j, c].astype(jnp.float32)
            for t in range(2):
                base = pl.multiple_of((target[t] // PACK) * PACK, PACK)
                block = buf[j, c, pl.ds(base, PACK), :].astype(jnp.float32)
                hit = sub + base == target[t]
                buf[j, c, pl.ds(base, PACK), :] = jnp.where(hit, fresh[t:t + 1], block).astype(buf.dtype)
        pltpu.make_async_copy(buf.at[j], out_ref.at[j], out_sem.at[j]).start()

    @pl.loop(0, stayed)
    def _(j):
        pltpu.make_async_copy(local_ref.at[0], heads_ref.at[j], heads_in.at[j]).wait()
        pltpu.make_async_copy(heads_ref.at[j], heads_out.at[j], heads_sem.at[j]).start()

    load_q.wait()
    for k in range(0, len(OFFSETS), 2):

        @pl.when(stayed + k < filled)
        def _(k=k):
            for e in range(2):

                @pl.when(stayed + k + e < filled)
                def _(e=e):
                    pltpu.make_async_copy(arrived_ref.at[0], raw.at[k + e], raw_sem.at[k + e]).wait()

            for e in range(2):
                j = jnp.minimum(stayed + k + e, filled - 1)
                position = place_pos[j]
                target = [SINK + lax.rem(position + t, window) for t in range(2)]
                attend(q_ref[j], lambda c: fresh_ref[j, c], lambda lanes: raw[k + e, 0, :, lanes],
                       lambda lanes: raw[k + e, 1, :, lanes], target, q_rows.at[e], o_rows.at[e])
            for e in range(2):

                @pl.when(stayed + k + e < filled)
                def _(e=e):
                    j = stayed + k + e
                    put_heads(heads_ref, j, o_rows.at[e])
                    pltpu.make_async_copy(heads_ref.at[j], heads_out.at[j], heads_sem.at[j]).start()

    @pl.loop(0, slots)
    def _(j):
        pltpu.make_async_copy(zeros, out_ref.at[j], out_sem.at[j]).wait()
        pltpu.make_async_copy(heads_ref.at[j], heads_out.at[j], heads_sem.at[j]).wait()


def decode(n, counts, hops, pos, table, kv, arrived, queries, fresh, local):
    smem = pl.BlockSpec(memory_space=pltpu.SMEM)
    hbm = pl.BlockSpec(memory_space=pl.ANY)
    dma = pltpu.SemaphoreType.DMA
    slots = kv.shape[0]
    heads = queries.shape[-1] // HEAD_DIM
    return pl.pallas_call(
        functools.partial(decode_kernel, n),
        out_shape=(jax.ShapeDtypeStruct(kv.shape, kv.dtype),
                   jax.ShapeDtypeStruct(queries.shape, queries.dtype),
                   jax.ShapeDtypeStruct((n,), jnp.int32)),
        in_specs=[smem, smem, smem, smem, hbm, hbm, hbm, hbm, hbm],
        out_specs=(hbm, hbm, smem),
        scratch_shapes=[pltpu.VMEM(kv.shape, kv.dtype),
                        pltpu.VMEM(arrived.shape, kv.dtype),
                        pltpu.VMEM(kv.shape[1:], kv.dtype),
                        pltpu.VMEM(queries.shape, queries.dtype),
                        pltpu.VMEM(fresh.shape, fresh.dtype),
                        pltpu.VMEM(queries.shape, queries.dtype),
                        pltpu.VMEM((2, 2 * heads, HEAD_DIM), jnp.float32),
                        pltpu.VMEM((2, 2 * heads, HEAD_DIM), jnp.float32),
                        pltpu.SMEM((slots,), jnp.int32),
                        dma((slots,)), dma((len(OFFSETS),)), dma((slots,)),
                        dma((2,)), dma((slots,)), dma((slots,))],
        name="decode",
    )(counts, hops, pos, table, kv, arrived, queries, fresh, local)


def solution(mesh):
    n = mesh.shape["grp"]

    def per_device(counts, hop_offsets, write_pos, kv_cache, queries, fresh_kv):
        arrived, table, local = exchange(n, counts, hop_offsets, write_pos, kv_cache, queries, fresh_kv)
        return decode(n, counts, hop_offsets, write_pos, table, kv_cache, arrived, queries, fresh_kv, local)

    return jax.shard_map(
        per_device,
        mesh=mesh,
        in_specs=(
            P(("rep", "grp")),
            P(("rep", "grp")),
            P(("rep", "grp")),
            P(("rep", "grp"), None, None, "tp"),
            P(("rep", "grp"), None, "tp"),
            P(("rep", "grp"), None, None, "tp"),
        ),
        out_specs=(P(("rep", "grp"), None, None, "tp"), P(("rep", "grp"), None, "tp"), P("rep")),
        check_vma=False,
    )
```

```python
import functools

import jax
import jax.numpy as jnp
from jax import lax
from jax.experimental import pallas as pl
from jax.experimental.pallas import tpu as pltpu
from jax.sharding import PartitionSpec as P

HEAD_DIM = 128
SINK = 4
OFFSETS = (-2, -1, 1, 2)
PACK = 16


def attend(pair, fresh_of, keys_of, values_of, target, q_rows, o_rows):
    heads = pair.shape[-1] // HEAD_DIM
    q = pair.astype(jnp.float32)
    for h in range(heads):
        q_rows[2 * h:2 * h + 2] = q[:, h * HEAD_DIM:(h + 1) * HEAD_DIM]
    fresh = [fresh_of(c).astype(jnp.float32) for c in range(2)]
    kv_heads = fresh[0].shape[-1] // HEAD_DIM
    rows = 2 * heads // kv_heads
    for g in range(kv_heads):
        lanes = slice(g * HEAD_DIM, (g + 1) * HEAD_DIM)
        query = q_rows[g * rows:(g + 1) * rows]
        keys, values = keys_of(lanes), values_of(lanes)
        column = lax.broadcasted_iota(jnp.int32, (rows, keys.shape[0]), 1)
        second = lax.rem(lax.broadcasted_iota(jnp.int32, (rows, keys.shape[0]), 0), 2) == 1
        hits = [column == target[0], (column == target[1]) & second]
        scores = lax.dot_general(query.astype(jnp.bfloat16), keys, (((1,), (1,)), ((), ())),
                                 preferred_element_type=jnp.float32)
        for t in range(2):
            now = jnp.sum(query * fresh[0][t:t + 1, lanes], axis=1, keepdims=True)
            scores = jnp.where(hits[t], now, scores)
        scores = scores * HEAD_DIM ** -0.5
        raised = jnp.exp(scores - jnp.max(scores, axis=1, keepdims=True))
        weights = (raised / jnp.sum(raised, axis=1, keepdims=True)).astype(jnp.bfloat16)
        wide = weights.astype(jnp.float32)
        kept = jnp.where(hits[0] | hits[1], 0.0, wide).astype(jnp.bfloat16)
        mixed = lax.dot_general(kept, values, (((1,), (0,)), ((), ())),
                                preferred_element_type=jnp.float32)
        for t in range(2):
            share = jnp.sum(jnp.where(hits[t], wide, 0.0), axis=1, keepdims=True)
            mixed = mixed + share * fresh[1][t:t + 1, lanes]
        o_rows[g * rows:(g + 1) * rows] = mixed


def put_heads(ref, j, o_rows):
    for h in range(ref.shape[-1] // HEAD_DIM):
        ref[j, :, h * HEAD_DIM:(h + 1) * HEAD_DIM] = o_rows[2 * h:2 * h + 2].astype(ref.dtype)


def exchange_kernel(n, counts_ref, hops_ref, pos_ref, kv_hbm, q_hbm, fresh_hbm, arrived_ref, table_ref, local_ref,
                    kv_ref, q_ref, fresh_ref, staged, meta, q_rows, o_rows, dest, load_sem, send_sem, recv_sem, meta_send, meta_recv,
                    own_sem):
    me = lax.axis_index("grp")
    slots = kv_ref.shape[0]
    barrier = pltpu.get_barrier_semaphore()

    @pl.loop(1, n)
    def _(k):
        pl.semaphore_signal(barrier, inc=1, device_id={"grp": lax.rem(me + k, n)})

    load = pltpu.make_async_copy(kv_hbm, kv_ref, load_sem.at[0])
    load.start()
    others = [pltpu.make_async_copy(q_hbm, q_ref, load_sem.at[1]),
              pltpu.make_async_copy(fresh_hbm, fresh_ref, load_sem.at[2])]
    for other in others:
        other.start()
    live = counts_ref[0]
    stay = jnp.int32(0)
    picked = [jnp.int32(0) for _ in OFFSETS]
    position = [jnp.int32(-1) for _ in OFFSETS]
    for s in range(slots):
        hop = jnp.where(s < live, hops_ref[s], 0)
        dest[s] = stay
        stay = stay + jnp.where((s < live) & (hop == 0), 1, 0)
        for i, offset in enumerate(OFFSETS):
            hit = hop == offset
            picked[i] = jnp.where(hit, s, picked[i])
            position[i] = jnp.where(hit, pos_ref[s], position[i])
    lane = lax.broadcasted_iota(jnp.int32, (1, 128), 1)
    row = jnp.where(lane == 0, stay, 0)
    for i in range(len(OFFSETS)):
        row = jnp.where(lane == 1 + i, position[i], row)
    meta[...] = row
    load.wait()
    for i in range(len(OFFSETS)):
        staged[i] = kv_ref[picked[i]]

    pl.semaphore_wait(barrier, n - 1)

    def meta_copy(k):
        return pltpu.make_async_remote_copy(
            src_ref=meta, dst_ref=table_ref.at[me], send_sem=meta_send.at[k],
            recv_sem=meta_recv.at[k], device_id={"grp": lax.rem(me + k, n)})

    copies = []
    for i, offset in enumerate(OFFSETS):
        copies.append(pltpu.make_async_remote_copy(
            src_ref=staged.at[i], dst_ref=arrived_ref.at[i], send_sem=send_sem.at[i],
            recv_sem=recv_sem.at[i], device_id={"grp": lax.rem(me + offset + n, n)}))

    @pl.loop(1, n)
    def _(k):
        meta_copy(k).start()

    for i in (0, 3, 1, 2):
        copies[i].start()
    own = pltpu.make_async_copy(meta, table_ref.at[me], own_sem)
    own.start()
    for other in others:
        other.wait()
    window = kv_ref.shape[2] - SINK

    @pl.loop(0, slots)
    def _(s):
        at = jnp.minimum(dest[s], slots - 1)
        position = pos_ref[s]
        target = [SINK + lax.rem(position + t, window) for t in range(2)]
        attend(q_ref[at], lambda c: fresh_ref[at, c], lambda lanes: kv_ref[s, 0, :, lanes],
               lambda lanes: kv_ref[s, 1, :, lanes], target, q_rows, o_rows)
        put_heads(local_ref, s, o_rows)

    own.wait()

    @pl.loop(1, n)
    def _(k):
        meta_copy(k).wait()

    for copy in copies:
        copy.wait()


def exchange(n, counts, hops, pos, kv, queries, fresh):
    many = len(OFFSETS)
    heads = queries.shape[-1] // HEAD_DIM
    smem = pl.BlockSpec(memory_space=pltpu.SMEM)
    vmem = pl.BlockSpec(memory_space=pltpu.VMEM)
    hbm = pl.BlockSpec(memory_space=pl.ANY)
    dma = pltpu.SemaphoreType.DMA
    return pl.pallas_call(
        functools.partial(exchange_kernel, n),
        out_shape=(jax.ShapeDtypeStruct((many,) + kv.shape[1:], kv.dtype),
                   jax.ShapeDtypeStruct((n, 1, 128), jnp.int32),
                   jax.ShapeDtypeStruct(queries.shape, queries.dtype)),
        in_specs=[smem, smem, smem, hbm, hbm, hbm],
        out_specs=(hbm, hbm, vmem),
        scratch_shapes=[pltpu.VMEM(kv.shape, kv.dtype),
                        pltpu.VMEM(queries.shape, queries.dtype),
                        pltpu.VMEM(fresh.shape, fresh.dtype),
                        pltpu.VMEM((many,) + kv.shape[1:], kv.dtype),
                        pltpu.VMEM((1, 128), jnp.int32),
                        pltpu.VMEM((2 * heads, HEAD_DIM), jnp.float32),
                        pltpu.VMEM((2 * heads, HEAD_DIM), jnp.float32),
                        pltpu.SMEM((kv.shape[0],), jnp.int32),
                        dma((3,)), dma((many,)), dma((many,)), dma((n,)), dma((n,)), dma(())],
        compiler_params=pltpu.CompilerParams(collective_id=0, has_side_effects=True),
        name="exchange",
    )(counts, hops, pos, kv, queries, fresh)


def decode_kernel(n, counts_ref, hops_ref, pos_ref, table_ref, kv_ref, arrived_ref, q_hbm, fresh_hbm, local_ref,
                  out_ref, heads_out, served_ref,
                  buf, raw, zeros, q_ref, fresh_ref, heads_ref, q_rows, o_rows, place_pos,
                  in_sem, raw_sem, out_sem, load_sem, heads_in, heads_sem):
    me = lax.axis_index("grp")
    slots, _, cache_len, width = kv_ref.shape
    window = cache_len - SINK

    load_fresh = pltpu.make_async_copy(fresh_hbm, fresh_ref, load_sem.at[0])
    load_q = pltpu.make_async_copy(q_hbm, q_ref, load_sem.at[1])
    load_fresh.start()
    live = counts_ref[0]
    filled = jnp.int32(0)
    for s in range(slots):
        stays = (s < live) & (hops_ref[s] == 0)

        @pl.when(stays)
        def _(s=s, at=filled):
            place_pos[at] = pos_ref[s]
            pltpu.make_async_copy(kv_ref.at[s], buf.at[at], in_sem.at[at]).start()
            pltpu.make_async_copy(local_ref.at[s], heads_ref.at[at], heads_in.at[at]).start()

        filled = filled + jnp.where(stays, 1, 0)
    stayed = filled
    for i, offset in enumerate(OFFSETS):
        position = table_ref[lax.rem(me - offset + n, n), 0, 1 + i]
        present = position >= 0

        @pl.when(present)
        def _(i=i, at=filled, position=position):
            place_pos[at] = position
            pltpu.make_async_copy(arrived_ref.at[i], buf.at[at], in_sem.at[at]).start()
            pltpu.make_async_copy(arrived_ref.at[i], raw.at[at - stayed], raw_sem.at[at - stayed]).start()

        filled = filled + jnp.where(present, 1, 0)

    load_q.start()
    zeros[...] = jnp.zeros_like(zeros)

    @pl.loop(0, n)
    def _(g):
        total = table_ref[g, 0, 0]
        for i, offset in enumerate(OFFSETS):
            total = total + jnp.where(table_ref[lax.rem(g - offset + n, n), 0, 1 + i] >= 0, 1, 0)
        served_ref[g] = total

    @pl.loop(filled, slots)
    def _(j):
        heads_ref[j] = jnp.zeros(heads_ref.shape[1:], heads_ref.dtype)
        pltpu.make_async_copy(heads_ref.at[j], heads_out.at[j], heads_sem.at[j]).start()
        pltpu.make_async_copy(zeros, out_ref.at[j], out_sem.at[j]).start()

    load_fresh.wait()
    sub = lax.broadcasted_iota(jnp.int32, (PACK, width), 0)

    @pl.loop(0, filled)
    def _(j):
        pltpu.make_async_copy(kv_ref.at[0], buf.at[j], in_sem.at[j]).wait()
        position = place_pos[j]
        target = [SINK + lax.rem(position + t, window) for t in range(2)]
        for c in range(2):
            fresh = fresh_ref[j, c].astype(jnp.float32)
            for t in range(2):
                base = pl.multiple_of((target[t] // PACK) * PACK, PACK)
                block = buf[j, c, pl.ds(base, PACK), :].astype(jnp.float32)
                hit = sub + base == target[t]
                buf[j, c, pl.ds(base, PACK), :] = jnp.where(hit, fresh[t:t + 1], block).astype(buf.dtype)
        pltpu.make_async_copy(buf.at[j], out_ref.at[j], out_sem.at[j]).start()

    @pl.loop(0, stayed)
    def _(j):
        pltpu.make_async_copy(local_ref.at[0], heads_ref.at[j], heads_in.at[j]).wait()
        pltpu.make_async_copy(heads_ref.at[j], heads_out.at[j], heads_sem.at[j]).start()

    load_q.wait()

    @pl.loop(stayed, filled)
    def _(j):
        k = j - stayed
        pltpu.make_async_copy(arrived_ref.at[0], raw.at[k], raw_sem.at[k]).wait()
        position = place_pos[j]
        target = [SINK + lax.rem(position + t, window) for t in range(2)]
        attend(q_ref[j], lambda c: fresh_ref[j, c], lambda lanes: raw[k, 0, :, lanes],
               lambda lanes: raw[k, 1, :, lanes], target, q_rows, o_rows)
        put_heads(heads_ref, j, o_rows)
        pltpu.make_async_copy(heads_ref.at[j], heads_out.at[j], heads_sem.at[j]).start()

    @pl.loop(0, slots)
    def _(j):
        pltpu.make_async_copy(zeros, out_ref.at[j], out_sem.at[j]).wait()
        pltpu.make_async_copy(heads_ref.at[j], heads_out.at[j], heads_sem.at[j]).wait()


def decode(n, counts, hops, pos, table, kv, arrived, queries, fresh, local):
    smem = pl.BlockSpec(memory_space=pltpu.SMEM)
    hbm = pl.BlockSpec(memory_space=pl.ANY)
    dma = pltpu.SemaphoreType.DMA
    slots = kv.shape[0]
    heads = queries.shape[-1] // HEAD_DIM
    return pl.pallas_call(
        functools.partial(decode_kernel, n),
        out_shape=(jax.ShapeDtypeStruct(kv.shape, kv.dtype),
                   jax.ShapeDtypeStruct(queries.shape, queries.dtype),
                   jax.ShapeDtypeStruct((n,), jnp.int32)),
        in_specs=[smem, smem, smem, smem, hbm, hbm, hbm, hbm, hbm],
        out_specs=(hbm, hbm, smem),
        scratch_shapes=[pltpu.VMEM(kv.shape, kv.dtype),
                        pltpu.VMEM(arrived.shape, kv.dtype),
                        pltpu.VMEM(kv.shape[1:], kv.dtype),
                        pltpu.VMEM(queries.shape, queries.dtype),
                        pltpu.VMEM(fresh.shape, fresh.dtype),
                        pltpu.VMEM(queries.shape, queries.dtype),
                        pltpu.VMEM((2 * heads, HEAD_DIM), jnp.float32),
                        pltpu.VMEM((2 * heads, HEAD_DIM), jnp.float32),
                        pltpu.SMEM((slots,), jnp.int32),
                        dma((slots,)), dma((len(OFFSETS),)), dma((slots,)),
                        dma((2,)), dma((slots,)), dma((slots,))],
        name="decode",
    )(counts, hops, pos, table, kv, arrived, queries, fresh, local)


def solution(mesh):
    n = mesh.shape["grp"]

    def per_device(counts, hop_offsets, write_pos, kv_cache, queries, fresh_kv):
        arrived, table, local = exchange(n, counts, hop_offsets, write_pos, kv_cache, queries, fresh_kv)
        return decode(n, counts, hop_offsets, write_pos, table, kv_cache, arrived, queries, fresh_kv, local)

    return jax.shard_map(
        per_device,
        mesh=mesh,
        in_specs=(
            P(("rep", "grp")),
            P(("rep", "grp")),
            P(("rep", "grp")),
            P(("rep", "grp"), None, None, "tp"),
            P(("rep", "grp"), None, "tp"),
            P(("rep", "grp"), None, None, "tp"),
        ),
        out_specs=(P(("rep", "grp"), None, None, "tp"), P(("rep", "grp"), None, "tp"), P("rep")),
        check_vma=False,
    )
```

```python
import functools

import jax
import jax.numpy as jnp
from jax import lax
from jax.experimental import pallas as pl
from jax.experimental.pallas import tpu as pltpu
from jax.sharding import PartitionSpec as P

HEAD_DIM = 128
SINK = 4
OFFSETS = (-2, -1, 1, 2)
PACK = 16


def attend(pair, fresh_of, keys_of, values_of, target, q_rows, o_rows):
    heads = pair.shape[-1] // HEAD_DIM
    q = pair.astype(jnp.float32)
    for h in range(heads):
        q_rows[2 * h:2 * h + 2] = q[:, h * HEAD_DIM:(h + 1) * HEAD_DIM]
    fresh = [fresh_of(c).astype(jnp.float32) for c in range(2)]
    kv_heads = fresh[0].shape[-1] // HEAD_DIM
    rows = 2 * heads // kv_heads
    for g in range(kv_heads):
        lanes = slice(g * HEAD_DIM, (g + 1) * HEAD_DIM)
        query = q_rows[g * rows:(g + 1) * rows]
        keys, values = keys_of(lanes), values_of(lanes)
        column = lax.broadcasted_iota(jnp.int32, (rows, keys.shape[0]), 1)
        second = lax.rem(lax.broadcasted_iota(jnp.int32, (rows, keys.shape[0]), 0), 2) == 1
        hits = [column == target[0], (column == target[1]) & second]
        scores = lax.dot_general(query.astype(jnp.bfloat16), keys, (((1,), (1,)), ((), ())),
                                 preferred_element_type=jnp.float32)
        for t in range(2):
            now = jnp.sum(query * fresh[0][t:t + 1, lanes], axis=1, keepdims=True)
            scores = jnp.where(hits[t], now, scores)
        scores = scores * HEAD_DIM ** -0.5
        raised = jnp.exp(scores - jnp.max(scores, axis=1, keepdims=True))
        weights = (raised / jnp.sum(raised, axis=1, keepdims=True)).astype(jnp.bfloat16)
        wide = weights.astype(jnp.float32)
        kept = jnp.where(hits[0] | hits[1], 0.0, wide).astype(jnp.bfloat16)
        mixed = lax.dot_general(kept, values, (((1,), (0,)), ((), ())),
                                preferred_element_type=jnp.float32)
        for t in range(2):
            share = jnp.sum(jnp.where(hits[t], wide, 0.0), axis=1, keepdims=True)
            mixed = mixed + share * fresh[1][t:t + 1, lanes]
        o_rows[g * rows:(g + 1) * rows] = mixed


def put_heads(ref, j, o_rows):
    for h in range(ref.shape[-1] // HEAD_DIM):
        ref[j, :, h * HEAD_DIM:(h + 1) * HEAD_DIM] = o_rows[2 * h:2 * h + 2].astype(ref.dtype)


def exchange_kernel(n, counts_ref, hops_ref, pos_ref, kv_hbm, q_hbm, fresh_hbm, arrived_ref, table_ref, local_ref,
                    kv_ref, q_ref, fresh_ref, staged, meta, q_rows, o_rows, dest, load_sem, send_sem, recv_sem, meta_send, meta_recv,
                    own_sem):
    me = lax.axis_index("grp")
    slots = kv_ref.shape[0]
    barrier = pltpu.get_barrier_semaphore()

    @pl.loop(1, n)
    def _(k):
        pl.semaphore_signal(barrier, inc=1, device_id={"grp": lax.rem(me + k, n)})

    load = pltpu.make_async_copy(kv_hbm, kv_ref, load_sem.at[0])
    load.start()
    others = [pltpu.make_async_copy(q_hbm, q_ref, load_sem.at[1]),
              pltpu.make_async_copy(fresh_hbm, fresh_ref, load_sem.at[2])]
    for other in others:
        other.start()
    live = counts_ref[0]
    stay = jnp.int32(0)
    picked = [jnp.int32(0) for _ in OFFSETS]
    position = [jnp.int32(-1) for _ in OFFSETS]
    for s in range(slots):
        hop = jnp.where(s < live, hops_ref[s], 0)
        dest[s] = stay
        stay = stay + jnp.where((s < live) & (hop == 0), 1, 0)
        for i, offset in enumerate(OFFSETS):
            hit = hop == offset
            picked[i] = jnp.where(hit, s, picked[i])
            position[i] = jnp.where(hit, pos_ref[s], position[i])
    lane = lax.broadcasted_iota(jnp.int32, (1, 128), 1)
    row = jnp.where(lane == 0, stay, 0)
    for i in range(len(OFFSETS)):
        row = jnp.where(lane == 1 + i, position[i], row)
    meta[...] = row
    load.wait()
    for i in range(len(OFFSETS)):
        staged[i] = kv_ref[picked[i]]

    pl.semaphore_wait(barrier, n - 1)

    def meta_copy(k):
        return pltpu.make_async_remote_copy(
            src_ref=meta, dst_ref=table_ref.at[me], send_sem=meta_send.at[k],
            recv_sem=meta_recv.at[k], device_id={"grp": lax.rem(me + k, n)})

    copies = []
    for i, offset in enumerate(OFFSETS):
        copies.append(pltpu.make_async_remote_copy(
            src_ref=staged.at[i], dst_ref=arrived_ref.at[i], send_sem=send_sem.at[i],
            recv_sem=recv_sem.at[i], device_id={"grp": lax.rem(me + offset + n, n)}))

    @pl.loop(1, n)
    def _(k):
        meta_copy(k).start()

    lower = me < n // 2

    @pl.when(lower)
    def _():
        for i in (0, 1, 3, 2):
            copies[i].start()

    @pl.when(jnp.logical_not(lower))
    def _():
        for i in (3, 2, 0, 1):
            copies[i].start()

    own = pltpu.make_async_copy(meta, table_ref.at[me], own_sem)
    own.start()
    for other in others:
        other.wait()
    window = kv_ref.shape[2] - SINK

    @pl.loop(0, slots)
    def _(s):
        at = jnp.minimum(dest[s], slots - 1)
        position = pos_ref[s]
        target = [SINK + lax.rem(position + t, window) for t in range(2)]
        attend(q_ref[at], lambda c: fresh_ref[at, c], lambda lanes: kv_ref[s, 0, :, lanes],
               lambda lanes: kv_ref[s, 1, :, lanes], target, q_rows, o_rows)
        put_heads(local_ref, s, o_rows)

    own.wait()

    @pl.loop(1, n)
    def _(k):
        meta_copy(k).wait()

    for copy in copies:
        copy.wait()


def exchange(n, counts, hops, pos, kv, queries, fresh):
    many = len(OFFSETS)
    heads = queries.shape[-1] // HEAD_DIM
    smem = pl.BlockSpec(memory_space=pltpu.SMEM)
    vmem = pl.BlockSpec(memory_space=pltpu.VMEM)
    hbm = pl.BlockSpec(memory_space=pl.ANY)
    dma = pltpu.SemaphoreType.DMA
    return pl.pallas_call(
        functools.partial(exchange_kernel, n),
        out_shape=(jax.ShapeDtypeStruct((many,) + kv.shape[1:], kv.dtype),
                   jax.ShapeDtypeStruct((n, 1, 128), jnp.int32),
                   jax.ShapeDtypeStruct(queries.shape, queries.dtype)),
        in_specs=[smem, smem, smem, hbm, hbm, hbm],
        out_specs=(hbm, hbm, vmem),
        scratch_shapes=[pltpu.VMEM(kv.shape, kv.dtype),
                        pltpu.VMEM(queries.shape, queries.dtype),
                        pltpu.VMEM(fresh.shape, fresh.dtype),
                        pltpu.VMEM((many,) + kv.shape[1:], kv.dtype),
                        pltpu.VMEM((1, 128), jnp.int32),
                        pltpu.VMEM((2 * heads, HEAD_DIM), jnp.float32),
                        pltpu.VMEM((2 * heads, HEAD_DIM), jnp.float32),
                        pltpu.SMEM((kv.shape[0],), jnp.int32),
                        dma((3,)), dma((many,)), dma((many,)), dma((n,)), dma((n,)), dma(())],
        compiler_params=pltpu.CompilerParams(collective_id=0, has_side_effects=True),
        name="exchange",
    )(counts, hops, pos, kv, queries, fresh)


def decode_kernel(n, counts_ref, hops_ref, pos_ref, table_ref, kv_ref, arrived_ref, q_hbm, fresh_hbm, local_ref,
                  out_ref, heads_out, served_ref,
                  buf, raw, zeros, q_ref, fresh_ref, heads_ref, q_rows, o_rows, place_pos,
                  in_sem, raw_sem, out_sem, load_sem, heads_in, heads_sem):
    me = lax.axis_index("grp")
    slots, _, cache_len, width = kv_ref.shape
    window = cache_len - SINK

    load_fresh = pltpu.make_async_copy(fresh_hbm, fresh_ref, load_sem.at[0])
    load_q = pltpu.make_async_copy(q_hbm, q_ref, load_sem.at[1])
    load_fresh.start()
    live = counts_ref[0]
    filled = jnp.int32(0)
    for s in range(slots):
        stays = (s < live) & (hops_ref[s] == 0)

        @pl.when(stays)
        def _(s=s, at=filled):
            place_pos[at] = pos_ref[s]
            pltpu.make_async_copy(kv_ref.at[s], buf.at[at], in_sem.at[at]).start()
            pltpu.make_async_copy(local_ref.at[s], heads_ref.at[at], heads_in.at[at]).start()

        filled = filled + jnp.where(stays, 1, 0)
    stayed = filled
    for i, offset in enumerate(OFFSETS):
        position = table_ref[lax.rem(me - offset + n, n), 0, 1 + i]
        present = position >= 0

        @pl.when(present)
        def _(i=i, at=filled, position=position):
            place_pos[at] = position
            pltpu.make_async_copy(arrived_ref.at[i], buf.at[at], in_sem.at[at]).start()
            pltpu.make_async_copy(arrived_ref.at[i], raw.at[at - stayed], raw_sem.at[at - stayed]).start()

        filled = filled + jnp.where(present, 1, 0)

    load_q.start()
    zeros[...] = jnp.zeros_like(zeros)

    @pl.loop(0, n)
    def _(g):
        total = table_ref[g, 0, 0]
        for i, offset in enumerate(OFFSETS):
            total = total + jnp.where(table_ref[lax.rem(g - offset + n, n), 0, 1 + i] >= 0, 1, 0)
        served_ref[g] = total

    @pl.loop(filled, slots)
    def _(j):
        heads_ref[j] = jnp.zeros(heads_ref.shape[1:], heads_ref.dtype)
        pltpu.make_async_copy(heads_ref.at[j], heads_out.at[j], heads_sem.at[j]).start()
        pltpu.make_async_copy(zeros, out_ref.at[j], out_sem.at[j]).start()

    load_fresh.wait()
    sub = lax.broadcasted_iota(jnp.int32, (PACK, width), 0)

    @pl.loop(0, filled)
    def _(j):
        pltpu.make_async_copy(kv_ref.at[0], buf.at[j], in_sem.at[j]).wait()
        position = place_pos[j]
        target = [SINK + lax.rem(position + t, window) for t in range(2)]
        for c in range(2):
            fresh = fresh_ref[j, c].astype(jnp.float32)
            for t in range(2):
                base = pl.multiple_of((target[t] // PACK) * PACK, PACK)
                block = buf[j, c, pl.ds(base, PACK), :].astype(jnp.float32)
                hit = sub + base == target[t]
                buf[j, c, pl.ds(base, PACK), :] = jnp.where(hit, fresh[t:t + 1], block).astype(buf.dtype)
        pltpu.make_async_copy(buf.at[j], out_ref.at[j], out_sem.at[j]).start()

    @pl.loop(0, stayed)
    def _(j):
        pltpu.make_async_copy(local_ref.at[0], heads_ref.at[j], heads_in.at[j]).wait()
        pltpu.make_async_copy(heads_ref.at[j], heads_out.at[j], heads_sem.at[j]).start()

    load_q.wait()

    @pl.loop(stayed, filled)
    def _(j):
        k = j - stayed
        pltpu.make_async_copy(arrived_ref.at[0], raw.at[k], raw_sem.at[k]).wait()
        position = place_pos[j]
        target = [SINK + lax.rem(position + t, window) for t in range(2)]
        attend(q_ref[j], lambda c: fresh_ref[j, c], lambda lanes: raw[k, 0, :, lanes],
               lambda lanes: raw[k, 1, :, lanes], target, q_rows, o_rows)
        put_heads(heads_ref, j, o_rows)
        pltpu.make_async_copy(heads_ref.at[j], heads_out.at[j], heads_sem.at[j]).start()

    @pl.loop(0, slots)
    def _(j):
        pltpu.make_async_copy(zeros, out_ref.at[j], out_sem.at[j]).wait()
        pltpu.make_async_copy(heads_ref.at[j], heads_out.at[j], heads_sem.at[j]).wait()


def decode(n, counts, hops, pos, table, kv, arrived, queries, fresh, local):
    smem = pl.BlockSpec(memory_space=pltpu.SMEM)
    hbm = pl.BlockSpec(memory_space=pl.ANY)
    dma = pltpu.SemaphoreType.DMA
    slots = kv.shape[0]
    heads = queries.shape[-1] // HEAD_DIM
    return pl.pallas_call(
        functools.partial(decode_kernel, n),
        out_shape=(jax.ShapeDtypeStruct(kv.shape, kv.dtype),
                   jax.ShapeDtypeStruct(queries.shape, queries.dtype),
                   jax.ShapeDtypeStruct((n,), jnp.int32)),
        in_specs=[smem, smem, smem, smem, hbm, hbm, hbm, hbm, hbm],
        out_specs=(hbm, hbm, smem),
        scratch_shapes=[pltpu.VMEM(kv.shape, kv.dtype),
                        pltpu.VMEM(arrived.shape, kv.dtype),
                        pltpu.VMEM(kv.shape[1:], kv.dtype),
                        pltpu.VMEM(queries.shape, queries.dtype),
                        pltpu.VMEM(fresh.shape, fresh.dtype),
                        pltpu.VMEM(queries.shape, queries.dtype),
                        pltpu.VMEM((2 * heads, HEAD_DIM), jnp.float32),
                        pltpu.VMEM((2 * heads, HEAD_DIM), jnp.float32),
                        pltpu.SMEM((slots,), jnp.int32),
                        dma((slots,)), dma((len(OFFSETS),)), dma((slots,)),
                        dma((2,)), dma((slots,)), dma((slots,))],
        name="decode",
    )(counts, hops, pos, table, kv, arrived, queries, fresh, local)


def solution(mesh):
    n = mesh.shape["grp"]

    def per_device(counts, hop_offsets, write_pos, kv_cache, queries, fresh_kv):
        arrived, table, local = exchange(n, counts, hop_offsets, write_pos, kv_cache, queries, fresh_kv)
        return decode(n, counts, hop_offsets, write_pos, table, kv_cache, arrived, queries, fresh_kv, local)

    return jax.shard_map(
        per_device,
        mesh=mesh,
        in_specs=(
            P(("rep", "grp")),
            P(("rep", "grp")),
            P(("rep", "grp")),
            P(("rep", "grp"), None, None, "tp"),
            P(("rep", "grp"), None, "tp"),
            P(("rep", "grp"), None, None, "tp"),
        ),
        out_specs=(P(("rep", "grp"), None, None, "tp"), P(("rep", "grp"), None, "tp"), P("rep")),
        check_vma=False,
    )
```

```python
import functools

import jax
import jax.numpy as jnp
from jax import lax
from jax.experimental import pallas as pl
from jax.experimental.pallas import tpu as pltpu
from jax.sharding import PartitionSpec as P

HEAD_DIM = 128
SINK = 4
OFFSETS = (-2, -1, 1, 2)
PACK = 16


def attend(pair, fresh_of, keys_of, values_of, target, q_rows, o_rows):
    heads = pair.shape[-1] // HEAD_DIM
    q = pair.astype(jnp.float32)
    for h in range(heads):
        q_rows[2 * h:2 * h + 2] = q[:, h * HEAD_DIM:(h + 1) * HEAD_DIM]
    fresh = [fresh_of(c).astype(jnp.float32) for c in range(2)]
    kv_heads = fresh[0].shape[-1] // HEAD_DIM
    rows = 2 * heads // kv_heads
    for g in range(kv_heads):
        lanes = slice(g * HEAD_DIM, (g + 1) * HEAD_DIM)
        query = q_rows[g * rows:(g + 1) * rows]
        keys, values = keys_of(lanes), values_of(lanes)
        column = lax.broadcasted_iota(jnp.int32, (rows, keys.shape[0]), 1)
        second = lax.rem(lax.broadcasted_iota(jnp.int32, (rows, keys.shape[0]), 0), 2) == 1
        hits = [column == target[0], (column == target[1]) & second]
        scores = lax.dot_general(query.astype(jnp.bfloat16), keys, (((1,), (1,)), ((), ())),
                                 preferred_element_type=jnp.float32)
        for t in range(2):
            now = jnp.sum(query * fresh[0][t:t + 1, lanes], axis=1, keepdims=True)
            scores = jnp.where(hits[t], now, scores)
        scores = scores * HEAD_DIM ** -0.5
        raised = jnp.exp(scores - jnp.max(scores, axis=1, keepdims=True))
        weights = (raised / jnp.sum(raised, axis=1, keepdims=True)).astype(jnp.bfloat16)
        wide = weights.astype(jnp.float32)
        kept = jnp.where(hits[0] | hits[1], 0.0, wide).astype(jnp.bfloat16)
        mixed = lax.dot_general(kept, values, (((1,), (0,)), ((), ())),
                                preferred_element_type=jnp.float32)
        for t in range(2):
            share = jnp.sum(jnp.where(hits[t], wide, 0.0), axis=1, keepdims=True)
            mixed = mixed + share * fresh[1][t:t + 1, lanes]
        o_rows[g * rows:(g + 1) * rows] = mixed


def put_heads(ref, j, o_rows):
    for h in range(ref.shape[-1] // HEAD_DIM):
        ref[j, :, h * HEAD_DIM:(h + 1) * HEAD_DIM] = o_rows[2 * h:2 * h + 2].astype(ref.dtype)


def exchange_kernel(n, counts_ref, hops_ref, pos_ref, kv_hbm, q_hbm, fresh_hbm, arrived_ref, table_ref, local_ref,
                    kv_ref, q_ref, fresh_ref, staged, meta, q_rows, o_rows, dest, load_sem, send_sem, recv_sem, meta_send, meta_recv,
                    own_sem):
    me = lax.axis_index("grp")
    slots = kv_ref.shape[0]
    barrier = pltpu.get_barrier_semaphore()

    @pl.loop(1, n)
    def _(k):
        pl.semaphore_signal(barrier, inc=1, device_id={"grp": lax.rem(me + k, n)})

    load = pltpu.make_async_copy(kv_hbm, kv_ref, load_sem.at[0])
    load.start()
    others = [pltpu.make_async_copy(q_hbm, q_ref, load_sem.at[1]),
              pltpu.make_async_copy(fresh_hbm, fresh_ref, load_sem.at[2])]
    for other in others:
        other.start()
    live = counts_ref[0]
    stay = jnp.int32(0)
    picked = [jnp.int32(0) for _ in OFFSETS]
    position = [jnp.int32(-1) for _ in OFFSETS]
    for s in range(slots):
        hop = jnp.where(s < live, hops_ref[s], 0)
        dest[s] = stay
        stay = stay + jnp.where((s < live) & (hop == 0), 1, 0)
        for i, offset in enumerate(OFFSETS):
            hit = hop == offset
            picked[i] = jnp.where(hit, s, picked[i])
            position[i] = jnp.where(hit, pos_ref[s], position[i])
    lane = lax.broadcasted_iota(jnp.int32, (1, 128), 1)
    row = jnp.where(lane == 0, stay, 0)
    for i in range(len(OFFSETS)):
        row = jnp.where(lane == 1 + i, position[i], row)
    meta[...] = row
    load.wait()
    for i in range(len(OFFSETS)):
        staged[i] = kv_ref[picked[i]]

    pl.semaphore_wait(barrier, n - 1)

    def meta_copy(k):
        return pltpu.make_async_remote_copy(
            src_ref=meta, dst_ref=table_ref.at[me], send_sem=meta_send.at[k],
            recv_sem=meta_recv.at[k], device_id={"grp": lax.rem(me + k, n)})

    copies = []
    for i, offset in enumerate(OFFSETS):
        copies.append(pltpu.make_async_remote_copy(
            src_ref=staged.at[i], dst_ref=arrived_ref.at[i], send_sem=send_sem.at[i],
            recv_sem=recv_sem.at[i], device_id={"grp": lax.rem(me + offset + n, n)}))

    @pl.loop(1, n)
    def _(k):
        meta_copy(k).start()

    lower = me < n // 2

    @pl.when(lower)
    def _():
        for i in (0, 1, 3, 2):
            copies[i].start()

    @pl.when(jnp.logical_not(lower))
    def _():
        for i in (3, 2, 0, 1):
            copies[i].start()

    own = pltpu.make_async_copy(meta, table_ref.at[me], own_sem)
    own.start()
    for other in others:
        other.wait()
    window = kv_ref.shape[2] - SINK

    @pl.loop(0, slots)
    def _(s):
        at = jnp.minimum(dest[s], slots - 1)
        position = pos_ref[s]
        target = [SINK + lax.rem(position + t, window) for t in range(2)]
        attend(q_ref[at], lambda c: fresh_ref[at, c], lambda lanes: kv_ref[s, 0, :, lanes],
               lambda lanes: kv_ref[s, 1, :, lanes], target, q_rows, o_rows)
        put_heads(local_ref, s, o_rows)

    own.wait()

    @pl.loop(1, n)
    def _(k):
        meta_copy(k).wait()

    for copy in copies:
        copy.wait()


def exchange(n, counts, hops, pos, kv, queries, fresh):
    many = len(OFFSETS)
    heads = queries.shape[-1] // HEAD_DIM
    smem = pl.BlockSpec(memory_space=pltpu.SMEM)
    vmem = pl.BlockSpec(memory_space=pltpu.VMEM)
    hbm = pl.BlockSpec(memory_space=pl.ANY)
    dma = pltpu.SemaphoreType.DMA
    return pl.pallas_call(
        functools.partial(exchange_kernel, n),
        out_shape=(jax.ShapeDtypeStruct((many,) + kv.shape[1:], kv.dtype),
                   jax.ShapeDtypeStruct((n, 1, 128), jnp.int32),
                   jax.ShapeDtypeStruct(queries.shape, queries.dtype)),
        in_specs=[smem, smem, smem, hbm, hbm, hbm],
        out_specs=(hbm, hbm, vmem),
        scratch_shapes=[pltpu.VMEM(kv.shape, kv.dtype),
                        pltpu.VMEM(queries.shape, queries.dtype),
                        pltpu.VMEM(fresh.shape, fresh.dtype),
                        pltpu.VMEM((many,) + kv.shape[1:], kv.dtype),
                        pltpu.VMEM((1, 128), jnp.int32),
                        pltpu.VMEM((2 * heads, HEAD_DIM), jnp.float32),
                        pltpu.VMEM((2 * heads, HEAD_DIM), jnp.float32),
                        pltpu.SMEM((kv.shape[0],), jnp.int32),
                        dma((3,)), dma((many,)), dma((many,)), dma((n,)), dma((n,)), dma(())],
        compiler_params=pltpu.CompilerParams(collective_id=0, has_side_effects=True),
        name="exchange",
    )(counts, hops, pos, kv, queries, fresh)


def decode_kernel(n, counts_ref, hops_ref, pos_ref, table_ref, kv_ref, arrived_ref, q_hbm, fresh_hbm, local_ref,
                  out_ref, heads_out, served_ref,
                  buf, raw, zeros, q_ref, fresh_ref, heads_ref, q_rows, o_rows, place_pos,
                  in_sem, raw_sem, out_sem, load_sem, heads_in, heads_sem):
    me = lax.axis_index("grp")
    slots, _, cache_len, width = kv_ref.shape
    window = cache_len - SINK

    load_fresh = pltpu.make_async_copy(fresh_hbm, fresh_ref, load_sem.at[0])
    load_q = pltpu.make_async_copy(q_hbm, q_ref, load_sem.at[1])
    load_fresh.start()
    load_q.start()
    live = counts_ref[0]
    filled = jnp.int32(0)
    for s in range(slots):
        stays = (s < live) & (hops_ref[s] == 0)

        @pl.when(stays)
        def _(s=s, at=filled):
            place_pos[at] = pos_ref[s]
            pltpu.make_async_copy(kv_ref.at[s], buf.at[at], in_sem.at[at]).start()
            pltpu.make_async_copy(local_ref.at[s], heads_ref.at[at], heads_in.at[at]).start()

        filled = filled + jnp.where(stays, 1, 0)
    stayed = filled
    for i, offset in enumerate(OFFSETS):
        position = table_ref[lax.rem(me - offset + n, n), 0, 1 + i]
        present = position >= 0

        @pl.when(present)
        def _(i=i, at=filled, position=position):
            place_pos[at] = position
            pltpu.make_async_copy(arrived_ref.at[i], buf.at[at], in_sem.at[at]).start()
            pltpu.make_async_copy(arrived_ref.at[i], raw.at[at - stayed], raw_sem.at[at - stayed]).start()

        filled = filled + jnp.where(present, 1, 0)

    zeros[...] = jnp.zeros_like(zeros)

    @pl.loop(0, n)
    def _(g):
        total = table_ref[g, 0, 0]
        for i, offset in enumerate(OFFSETS):
            total = total + jnp.where(table_ref[lax.rem(g - offset + n, n), 0, 1 + i] >= 0, 1, 0)
        served_ref[g] = total

    @pl.loop(filled, slots)
    def _(j):
        heads_ref[j] = jnp.zeros(heads_ref.shape[1:], heads_ref.dtype)
        pltpu.make_async_copy(heads_ref.at[j], heads_out.at[j], heads_sem.at[j]).start()
        pltpu.make_async_copy(zeros, out_ref.at[j], out_sem.at[j]).start()

    load_fresh.wait()
    sub = lax.broadcasted_iota(jnp.int32, (PACK, width), 0)

    @pl.loop(0, filled)
    def _(j):
        pltpu.make_async_copy(kv_ref.at[0], buf.at[j], in_sem.at[j]).wait()
        position = place_pos[j]
        target = [SINK + lax.rem(position + t, window) for t in range(2)]
        for c in range(2):
            fresh = fresh_ref[j, c].astype(jnp.float32)
            for t in range(2):
                base = pl.multiple_of((target[t] // PACK) * PACK, PACK)
                block = buf[j, c, pl.ds(base, PACK), :].astype(jnp.float32)
                hit = sub + base == target[t]
                buf[j, c, pl.ds(base, PACK), :] = jnp.where(hit, fresh[t:t + 1], block).astype(buf.dtype)
        pltpu.make_async_copy(buf.at[j], out_ref.at[j], out_sem.at[j]).start()

    @pl.loop(0, stayed)
    def _(j):
        pltpu.make_async_copy(local_ref.at[0], heads_ref.at[j], heads_in.at[j]).wait()
        pltpu.make_async_copy(heads_ref.at[j], heads_out.at[j], heads_sem.at[j]).start()

    load_q.wait()

    @pl.loop(stayed, filled)
    def _(j):
        k = j - stayed
        pltpu.make_async_copy(arrived_ref.at[0], raw.at[k], raw_sem.at[k]).wait()
        position = place_pos[j]
        target = [SINK + lax.rem(position + t, window) for t in range(2)]
        attend(q_ref[j], lambda c: fresh_ref[j, c], lambda lanes: raw[k, 0, :, lanes],
               lambda lanes: raw[k, 1, :, lanes], target, q_rows, o_rows)
        put_heads(heads_ref, j, o_rows)
        pltpu.make_async_copy(heads_ref.at[j], heads_out.at[j], heads_sem.at[j]).start()

    @pl.loop(0, slots)
    def _(j):
        pltpu.make_async_copy(zeros, out_ref.at[j], out_sem.at[j]).wait()
        pltpu.make_async_copy(heads_ref.at[j], heads_out.at[j], heads_sem.at[j]).wait()


def decode(n, counts, hops, pos, table, kv, arrived, queries, fresh, local):
    smem = pl.BlockSpec(memory_space=pltpu.SMEM)
    hbm = pl.BlockSpec(memory_space=pl.ANY)
    dma = pltpu.SemaphoreType.DMA
    slots = kv.shape[0]
    heads = queries.shape[-1] // HEAD_DIM
    return pl.pallas_call(
        functools.partial(decode_kernel, n),
        out_shape=(jax.ShapeDtypeStruct(kv.shape, kv.dtype),
                   jax.ShapeDtypeStruct(queries.shape, queries.dtype),
                   jax.ShapeDtypeStruct((n,), jnp.int32)),
        in_specs=[smem, smem, smem, smem, hbm, hbm, hbm, hbm, hbm],
        out_specs=(hbm, hbm, smem),
        scratch_shapes=[pltpu.VMEM(kv.shape, kv.dtype),
                        pltpu.VMEM(arrived.shape, kv.dtype),
                        pltpu.VMEM(kv.shape[1:], kv.dtype),
                        pltpu.VMEM(queries.shape, queries.dtype),
                        pltpu.VMEM(fresh.shape, fresh.dtype),
                        pltpu.VMEM(queries.shape, queries.dtype),
                        pltpu.VMEM((2 * heads, HEAD_DIM), jnp.float32),
                        pltpu.VMEM((2 * heads, HEAD_DIM), jnp.float32),
                        pltpu.SMEM((slots,), jnp.int32),
                        dma((slots,)), dma((len(OFFSETS),)), dma((slots,)),
                        dma((2,)), dma((slots,)), dma((slots,))],
        name="decode",
    )(counts, hops, pos, table, kv, arrived, queries, fresh, local)


def solution(mesh):
    n = mesh.shape["grp"]

    def per_device(counts, hop_offsets, write_pos, kv_cache, queries, fresh_kv):
        arrived, table, local = exchange(n, counts, hop_offsets, write_pos, kv_cache, queries, fresh_kv)
        return decode(n, counts, hop_offsets, write_pos, table, kv_cache, arrived, queries, fresh_kv, local)

    return jax.shard_map(
        per_device,
        mesh=mesh,
        in_specs=(
            P(("rep", "grp")),
            P(("rep", "grp")),
            P(("rep", "grp")),
            P(("rep", "grp"), None, None, "tp"),
            P(("rep", "grp"), None, "tp"),
            P(("rep", "grp"), None, None, "tp"),
        ),
        out_specs=(P(("rep", "grp"), None, None, "tp"), P(("rep", "grp"), None, "tp"), P("rep")),
        check_vma=False,
    )
```
